1024 devices in a mesh: dp: 16 (over z_hi, y), audio: 64 (over z_lo, x, core).
Axes of the slice: x: 8, y: 8, z: 8 (z_hi: 2, z_lo: 4; z = z_hi * 4 + z_lo), core: 2. Of those that a mesh axis runs over, the one named last changes fastest.
Arguments:
- waveform: float32 [16, 112640], P('dp', 'audio'), may hold values from -6 to 6
- lengths: int32 [16], P('dp'), may hold values from 28160 to 112640, as said below
- conv0_weight: float32 [10, 512], replicated, may hold values from -2 to 2
- norm0_gain: float32 [512], replicated, may hold values from 0.5 to 1.5
- norm0_shift: float32 [512], replicated, may hold values from -1.8 to 1.8
- conv1_weight: bfloat16 [3, 512, 512], replicated, may hold values from -0.15625 to 0.15625
- norm1_gain: float32 [512], replicated, may hold values from 0.25 to 1.75
- norm1_shift: float32 [512], replicated, may hold values from -1.8 to 1.8
- cotangent: bfloat16 [16, 11264, 512], P('dp', 'audio'), may hold values from -0.013671875 to 0.013671875
Outputs:
- features: bfloat16 [16, 11264, 512], P('dp', 'audio')
- conv1_grad: float32 [786432], P(('dp', 'audio'))
- small_grads: float32 [14, 512], replicated
The draws below stay inside these ranges and needn't reach their ends.
Inputs may be any that keep to these rules, and one draw needn't show every extreme that they name: `lengths`: window 0 is complete (112640 valid samples); each other window is complete or holds a valid prefix.
All inputs are finite; a program needn't handle non-finite values.
Results may differ from the reference program's by a relative error of at most 0.0055.
Values sent between devices are 32-bit elements; how exact they have to be, the bound alone decides.
No kernel may reach another device: no remote copies, remote signals or barrier semaphores. Data moves between devices by JAX's collectives and lax.ppermute only.
A program may use at most 32 MiB of HBM per device.

```python
import jax
import jax.numpy as jnp
from jax import lax

C = 512
WINDOWS = 16
SAMPLES = 112640
FRAMES = 11264


def draw_lengths(key, part):
    key_short, key_full = jax.random.split(jax.random.fold_in(key, 7))
    short = jax.random.randint(key_short, (WINDOWS,), SAMPLES // 4, SAMPLES + 1)
    complete = jax.random.randint(key_full, (WINDOWS,), 0, 3) == 0
    complete = jnp.logical_or(complete, jnp.arange(WINDOWS) == 0)
    return jnp.where(complete, SAMPLES, short).astype(jnp.int32)


def level_of(stream_key, extent, cuts, low, high):
    def one(axis_at, blocks):
        heights = jax.random.uniform(jax.random.fold_in(jax.random.fold_in(stream_key, 6), axis_at), (blocks,), jnp.float32, low / len(cuts), high / len(cuts))
        return jnp.repeat(jnp.exp(heights), extent[axis_at] // blocks).reshape((-1,) + (1,) * (len(extent) - axis_at - 1))

    gain = one(*cuts[0])
    for cut in cuts[1:]:
        gain = gain * one(*cut)
    return gain


def gaussian(rng, dims, deviation, bound, shards=(), kind=jnp.bfloat16):
    result = deviation * jax.random.normal(rng, dims, jnp.float32)
    if shards:
        result = result * level_of(rng, dims, shards, -0.22, 0.18)
    return jnp.clip(result, -bound, bound).astype(kind)


def setup_inputs(seed: int = 0) -> dict:
    splits = jax.random.split(jax.random.key(seed), 10)
    waveform = gaussian(splits[0], (WINDOWS, SAMPLES), 1.0, 6.0, ((0, 16), (1, 64)), jnp.float32)
    lengths = draw_lengths(jax.random.fold_in(splits[9], 71), 0)
    conv0_weight = gaussian(splits[2], (10, C), 10 ** -0.5, 2.0, (), jnp.float32)
    norm0_gain = jnp.clip(1.0 + 0.1 * jax.random.normal(splits[3], (C,), jnp.float32), 0.5, 1.5)
    norm0_shift = gaussian(splits[4], (C,), 0.3, 1.8, (), jnp.float32)
    conv1_weight = gaussian(splits[5], (3, C, C), (3 * C) ** -0.5, 0.15625)
    norm1_gain = jnp.clip(1.0 + 0.15 * jax.random.normal(splits[6], (C,), jnp.float32), 0.25, 1.75)
    norm1_shift = gaussian(splits[7], (C,), 0.3, 1.8, (), jnp.float32)
    cotangent = gaussian(splits[8], (WINDOWS, FRAMES, C), ((WINDOWS * FRAMES) ** -0.5), 0.013671875, ((0, 16), (1, 64)))
    return dict(waveform=waveform, lengths=lengths, conv0_weight=conv0_weight, norm0_gain=norm0_gain, norm0_shift=norm0_shift, conv1_weight=conv1_weight, norm1_gain=norm1_gain, norm1_shift=norm1_shift, cotangent=cotangent)


def norm_gelu(pre_act, gain_vec, shift_vec):
    average = lax.optimization_barrier(jnp.mean(pre_act, -1, keepdims=True))
    centred = pre_act - average
    variance = lax.optimization_barrier(jnp.mean(centred * centred, -1, keepdims=True))
    return jax.nn.gelu(centred * lax.rsqrt(variance + 1e-05) * gain_vec + shift_vec, approximate=False)

def encoder_step(extended, valid_mask, cot_float, conv0_weight, norm0_gain, norm0_shift, conv1_weight, norm1_gain, norm1_shift):
    count_rows = extended.shape[0]
    chans = conv1_weight.shape[2]
    rows_first = extended.shape[1] // 5
    first_frames = rows_first - 1
    frames_dev = (extended.shape[1] - 10) // 10
    blocks = extended.reshape(count_rows, rows_first, 5)
    patches_first = jnp.concatenate([blocks[:, :first_frames], blocks[:, 1:]], 2).reshape(count_rows * first_frames, 10)
    pre_first = jnp.dot(patches_first, conv0_weight, precision=lax.Precision.HIGHEST, preferred_element_type=jnp.float32).reshape(count_rows, first_frames, chans)
    act_float, back_first = jax.vjp(norm_gelu, pre_first, norm0_gain, norm0_shift)
    act_first = act_float.astype(jnp.bfloat16)
    frame_pairs = act_first[:, :2 * frames_dev].reshape(count_rows, frames_dev, 2 * chans)
    next_frame = act_first[:, 2::2]
    patches_second = jnp.concatenate([frame_pairs, next_frame], 2).reshape(count_rows * frames_dev, 3 * chans)
    kernel_mat = conv1_weight.reshape(3 * chans, chans)
    pre_second = jnp.dot(patches_second, kernel_mat, preferred_element_type=jnp.float32).reshape(count_rows, frames_dev, chans)

    def second_norm(pre_act, gain_vec, shift_vec):
        return norm_gelu(pre_act, gain_vec, shift_vec) * valid_mask[:, :, None]
    feat_float, back_second = jax.vjp(second_norm, pre_second, norm1_gain, norm1_shift)
    d_pre_second, d_gain_second, d_shift_second = back_second(cot_float)
    d_pre_second = d_pre_second.astype(jnp.bfloat16).reshape(count_rows * frames_dev, chans)
    grad_kernel = lax.dot_general(patches_second, d_pre_second, (((0,), (0,)), ((), ())), preferred_element_type=jnp.float32)
    d_patch = lax.dot_general(d_pre_second, kernel_mat, (((1,), (1,)), ((), ())), preferred_element_type=jnp.float32).reshape(count_rows, frames_dev, 3, chans)
    leading = d_patch[:, :, :2].reshape(count_rows, 2 * frames_dev, chans)
    d_act_first = jnp.concatenate([leading, jnp.zeros((count_rows, 1, chans), leading.dtype)], 1)
    d_act_first = d_act_first.at[:, 2::2].add(d_patch[:, :, 2])
    d_pre_first, d_gain_first, d_shift_first = back_first(d_act_first)
    grad_first = lax.dot_general(patches_first, d_pre_first.reshape(count_rows * first_frames, chans), (((0,), (0,)), ((), ())), precision=lax.Precision.HIGHEST, preferred_element_type=jnp.float32)
    small_terms = jnp.concatenate([grad_first, d_gain_first[None], d_shift_first[None], d_gain_second[None], d_shift_second[None]], 0)
    return (feat_float.astype(jnp.bfloat16), grad_kernel, small_terms)

def reference(waveform, lengths, conv0_weight, norm0_gain, norm0_shift, conv1_weight, norm1_gain, norm1_shift, cotangent):
    windows = waveform.shape[0]
    samples = waveform.shape[1]
    chans = conv1_weight.shape[2]
    frames = samples // 10
    positions = jnp.arange(samples, dtype=jnp.int32)
    cleaned = waveform * (positions[None, :] < lengths[:, None]).astype(jnp.float32)
    extended = jnp.concatenate([cleaned, jnp.zeros((windows, 10), jnp.float32)], 1)
    frame_pos = jnp.arange(frames, dtype=jnp.int32)
    valid_mask = (frame_pos[None, :] < (lengths // 10)[:, None]).astype(jnp.float32)

    def advance(totals, inputs):
        ext_part, mask_part, cot_part = inputs
        feat_part, grad_kernel, small_terms = encoder_step(ext_part, mask_part, cot_part.astype(jnp.float32), conv0_weight, norm0_gain, norm0_shift, conv1_weight, norm1_gain, norm1_shift)
        return ((totals[0] + grad_kernel, totals[1] + small_terms), feat_part)
    start = (jnp.zeros((3 * chans, chans), jnp.float32), jnp.zeros((14, chans), jnp.float32))
    totals, feats = lax.scan(advance, start, (extended.reshape(windows, 1, samples + 10), valid_mask.reshape(windows, 1, frames), cotangent.reshape(windows, 1, frames, chans)))
    return (feats.reshape(windows, frames, chans), totals[0].reshape(-1), totals[1])
```

```python
import functools

import jax
import jax.numpy as jnp
import numpy as np
from jax import lax
from jax.experimental import pallas as pl
from jax.experimental.pallas import tpu as pltpu
from jax.sharding import Mesh
from jax.sharding import PartitionSpec as P

SHAPE = (2, 8, 4, 8, 2)
AXES = ("zh", "y", "zl", "x", "core")
EPS = 1e-05
BF16, F32 = jnp.bfloat16, jnp.float32

LEVELS = (
    ((2, "y", 1), (0, "z", 1), (3, "y", 2), (1, "z", 2), (4, "y", 4), (5, "z", 4)),
    ((0, "z", 1), (2, "y", 1), (1, "z", 2), (3, "y", 2), (5, "z", 4), (4, "y", 4)),
)


def partners(step):
    route = []
    for i in range(int(np.prod(SHAPE))):
        zh, y, zl, x, core = (int(v) for v in np.unravel_index(i, SHAPE))
        at = {"z": zh * 4 + zl, "y": y, "x": x, "core": core}
        axis, distance = step(core)
        at[axis] ^= distance
        there = (at["z"] // 4, at["y"], at["z"] % 4, at["x"], at["core"])
        route.append((i, int(np.ravel_multi_index(there, SHAPE))))
    return route


def exchange(value, step):
    return lax.ppermute(value, AXES, partners(step))


def normal_cdf(v):
    return 0.5 + 0.5 * lax.erf(v * np.float32(0.5**0.5))


def normal_pdf(v):
    return jnp.exp(v * v * np.float32(-0.5)) * np.float32((2 * np.pi) ** -0.5)


def split_patches(x3_ref, rim_ref, odd_rows, even_last):
    value = x3_ref[...]
    row = lax.broadcasted_iota(jnp.int32, value.shape, 0)
    lane = lax.broadcasted_iota(jnp.int32, value.shape, 1)
    value = jnp.where(row == odd_rows - 1, value + rim_ref[0:1, :], value)
    value = jnp.where(row == even_last, value + rim_ref[1:2, :], value)
    high = value.astype(BF16).astype(F32)
    return jnp.where(lane < 20, high, value - high).astype(BF16)


def forward_kernel(
    frames,
    chunk,
    tab_ref,
    meta_ref,
    x3_ref,
    rim_ref,
    w3_ref,
    gain0_ref,
    shift0_ref,
    w1_ref,
    gain1_ref,
    shift1_ref,
    cot_ref,
    feat_ref,
    keep_ref,
    send_ref,
    d_ref,
    xhat_ref,
    slope_ref,
    rstd_ref,
    norm1_ref,
    pre0_ref,
    even_ref,
    patch_ref,
    pre1_ref,
    half_ref,
):
    chans = w1_ref.shape[1]
    rows = x3_ref.shape[0]
    xs = split_patches(x3_ref, rim_ref, frames, 2 * frames)
    w3 = w3_ref[...]
    w3 = w3 - jnp.mean(w3, -1, keepdims=True)
    high = w3.astype(BF16).astype(F32)
    tap = lax.broadcasted_iota(jnp.int32, w3.shape, 0)
    ws = jnp.where((tap >= 10) & (tap < 20), w3 - high, high).astype(BF16)
    pre0_ref[...] = jnp.dot(xs, ws, preferred_element_type=F32)
    gain0 = jnp.broadcast_to(gain0_ref[...], (chunk, chans))
    shift0 = jnp.broadcast_to(shift0_ref[...], (chunk, chans))
    for at in range(0, rows, chunk):
        centred = pre0_ref[at : at + chunk]
        rstd = lax.rsqrt(jnp.mean(centred * centred, -1, keepdims=True) + EPS)
        xhat = centred * rstd
        v = xhat * gain0 + shift0
        cdf = normal_cdf(v)
        xhat_ref[at : at + chunk] = xhat
        slope_ref[at : at + chunk] = cdf + v * normal_pdf(v)
        rstd_ref[at : at + chunk] = jnp.broadcast_to(rstd, (chunk, 128))
        act = v * cdf
        if at < frames:
            patch_ref[at : at + chunk, chans : 2 * chans] = act.astype(BF16)
        else:
            even_ref[at - frames : at - frames + chunk] = act
    for at in range(0, frames, chunk):
        patch_ref[at : at + chunk, :chans] = even_ref[at : at + chunk].astype(BF16)
        patch_ref[at : at + chunk, 2 * chans :] = even_ref[at + 1 : at + 1 + chunk].astype(BF16)
    pre1_ref[...] = jnp.dot(patch_ref[...], w1_ref[...], preferred_element_type=F32)
    gain1 = jnp.broadcast_to(gain1_ref[...], (chunk, chans))
    shift1 = jnp.broadcast_to(shift1_ref[...], (chunk, chans))
    sum_gain = jnp.zeros((chunk, chans), F32)
    sum_shift = jnp.zeros((chunk, chans), F32)
    half = chans // 2
    for at in range(0, frames, chunk):
        pre = pre1_ref[at : at + chunk]
        centred = pre - jnp.mean(pre, -1, keepdims=True)
        rstd = lax.rsqrt(jnp.mean(centred * centred, -1, keepdims=True) + EPS)
        xhat = centred * rstd
        v = xhat * gain1 + shift1
        cdf = normal_cdf(v)
        frame = at + lax.broadcasted_iota(jnp.int32, (chunk, chans), 0)
        valid = frame < meta_ref[0]
        feat_ref[at : at + chunk] = jnp.where(valid, v * cdf, 0.0).astype(BF16)
        dv = cot_ref[at : at + chunk].astype(F32) * (cdf + v * normal_pdf(v))
        dv = jnp.where(valid, dv, 0.0)
        sum_gain = sum_gain + dv * xhat
        sum_shift = sum_shift + dv
        dx = dv * gain1
        first = jnp.mean(dx, -1, keepdims=True)
        second = jnp.mean(dx * xhat, -1, keepdims=True)
        d = (rstd * (dx - first - xhat * second)).astype(BF16)
        d_ref[at : at + chunk] = d
        half_ref[0, at : at + chunk] = d[:, :half]
        half_ref[1, at : at + chunk] = d[:, half:]
    norm1_ref[0:1] = jnp.sum(sum_gain, 0, keepdims=True)
    norm1_ref[1:2] = jnp.sum(sum_shift, 0, keepdims=True)
    core = meta_ref[1]
    blocks, block_rows = keep_ref.shape[0], keep_ref.shape[1]
    step = 16
    for out_ref, side in ((send_ref, 1), (keep_ref, 0)):
        d_half = half_ref[core ^ side]
        for b in range(0, blocks, step):
            lanes = patch_ref[:, b * block_rows : (b + step) * block_rows]
            grad = lax.dot_general(lanes, d_half, (((0,), (0,)), ((), ())), preferred_element_type=F32)
            for i in range(step):
                out_ref[tab_ref[side, b + i]] = grad[i * block_rows : (i + 1) * block_rows]


def backward_kernel(
    frames,
    chunk,
    d_ref,
    w1_ref,
    xhat_ref,
    slope_ref,
    rstd_ref,
    gain0_ref,
    x3_ref,
    rim_ref,
    norm1_ref,
    small_ref,
    dact_ref,
    dhigh_ref,
    dlow_ref,
):
    chans = w1_ref.shape[1]
    rows = x3_ref.shape[0]

    def spread(tap):
        return lax.dot_general(
            d_ref[...],
            w1_ref[tap * chans : (tap + 1) * chans],
            (((1,), (1,)), ((), ())),
            preferred_element_type=F32,
        )

    dact_ref[:frames] = spread(1)
    dact_ref[frames : 2 * frames] = spread(0)
    dact_ref[2 * frames :] = jnp.zeros((rows - 2 * frames, chans), F32)
    dact_ref[frames + 1 : 2 * frames + 1] += spread(2)
    gain0 = jnp.broadcast_to(gain0_ref[...], (chunk, chans))
    sum_gain = jnp.zeros((chunk, chans), F32)
    sum_shift = jnp.zeros((chunk, chans), F32)
    for at in range(0, rows, chunk):
        xhat = xhat_ref[at : at + chunk]
        dv = dact_ref[at : at + chunk] * slope_ref[at : at + chunk]
        sum_gain = sum_gain + dv * xhat
        sum_shift = sum_shift + dv
        dx = dv * gain0
        first = jnp.mean(dx, -1, keepdims=True)
        second = jnp.mean(dx * xhat, -1, keepdims=True)
        d = rstd_ref[at : at + chunk, :1] * (dx - first - xhat * second)
        high = d.astype(BF16)
        dhigh_ref[at : at + chunk] = high
        dlow_ref[at : at + chunk] = (d - high.astype(F32)).astype(BF16)
    xs = split_patches(x3_ref, rim_ref, frames, 2 * frames)
    over_rows = (((0,), (0,)), ((), ()))
    by_high = lax.dot_general(xs, dhigh_ref[...], over_rows, preferred_element_type=F32)
    by_low = lax.dot_general(xs, dlow_ref[...], over_rows, preferred_element_type=F32)
    small_ref[...] = jnp.zeros_like(small_ref)
    small_ref[0:10] = by_high[0:10] + by_high[20:30] + by_low[0:10]
    small_ref[10:11] = jnp.sum(sum_gain, 0, keepdims=True)
    small_ref[11:12] = jnp.sum(sum_shift, 0, keepdims=True)
    small_ref[12:14] = norm1_ref[0:2]


VMEM = pl.BlockSpec(memory_space=pltpu.VMEM)
SMEM = pl.BlockSpec(memory_space=pltpu.SMEM)


def place_tables(block, core):
    v = lax.broadcasted_iota(jnp.int32, (1, 64), 1) ^ block
    tables = []
    for levels in LEVELS:
        place = jnp.zeros_like(v)
        for bit, _, _ in levels:
            place = place * 2 + ((v >> bit) & 1)
        tables.append(place)
    own = jnp.where(core == 0, tables[0], tables[1])
    other = jnp.where(core == 0, tables[1], tables[0])
    return jnp.concatenate([own, other], 0)


def shards(
    waveform,
    lengths,
    conv0_weight,
    norm0_gain,
    norm0_shift,
    conv1_weight,
    norm1_gain,
    norm1_shift,
    cotangent,
):
    zh, y, zl, x, core = (lax.axis_index(name) for name in AXES)
    position = (zl * 8 + x) * 2 + core
    samples_dev = waveform.shape[1]
    frames = samples_dev // 10
    chans = conv1_weight.shape[2]
    length = lengths[0]
    sample_pos = position * samples_dev + jnp.arange(samples_dev, dtype=jnp.int32)
    cleaned = jnp.where(sample_pos < length, waveform[0], 0.0)

    first = cleaned[:10]
    rim_odd = jnp.concatenate([jnp.zeros((5,), F32), first[:5]])
    rim = jnp.stack([jnp.tile(rim_odd, 3), jnp.tile(first, 3)])
    back = []
    for i in range(int(np.prod(SHAPE))):
        if i % 64:
            back.append((i, i - 1))
    rim = lax.ppermute(rim, AXES, back)

    odd = jnp.concatenate([cleaned[5:], jnp.zeros((5,), F32)]).reshape(frames, 10)
    even = cleaned.reshape(frames, 10)
    rows = 2 * frames + 16
    patches = jnp.concatenate([odd, even, jnp.zeros((16, 10), F32)], 0)
    x3 = jnp.concatenate([patches, patches, patches], 1)
    w3 = jnp.concatenate([conv0_weight, conv0_weight, conv0_weight], 0)

    block = ((zh * 8 + y) * 4) + zl
    tab = place_tables(block, core)
    meta = jnp.stack([length // 10 - position * frames, core]).astype(jnp.int32)
    w1 = conv1_weight.reshape(3 * chans, chans)
    half = chans // 2
    chunk = 16
    shape = jax.ShapeDtypeStruct
    features, keep, send, d, xhat, slope, rstd, norm1 = pl.pallas_call(
        functools.partial(forward_kernel, frames, chunk),
        out_shape=(
            shape((frames, chans), BF16),
            shape((64, 24, half), F32),
            shape((64, 24, half), F32),
            shape((frames, chans), BF16),
            shape((rows, chans), F32),
            shape((rows, chans), F32),
            shape((rows, 128), F32),
            shape((8, chans), F32),
        ),
        in_specs=[SMEM, SMEM] + [VMEM] * 9,
        out_specs=(VMEM,) * 8,
        scratch_shapes=[
            pltpu.VMEM((rows, chans), F32),
            pltpu.VMEM((rows - frames, chans), F32),
            pltpu.VMEM((frames, 3 * chans), BF16),
            pltpu.VMEM((frames, chans), F32),
            pltpu.VMEM((2, frames, half), BF16),
        ],
        compiler_params=pltpu.CompilerParams(vmem_limit_bytes=24 << 20),
        name="forward",
    )(
        tab,
        meta,
        x3,
        rim,
        w3,
        norm0_gain.reshape(1, chans),
        norm0_shift.reshape(1, chans),
        w1,
        norm1_gain.reshape(1, chans),
        norm1_shift.reshape(1, chans),
        cotangent[0],
    )
    received = lax.ppermute(send, "core", [(0, 1), (1, 0)])
    small = pl.pallas_call(
        functools.partial(backward_kernel, frames, chunk),
        out_shape=shape((16, chans), F32),
        in_specs=[VMEM] * 9,
        out_specs=VMEM,
        scratch_shapes=[
            pltpu.VMEM((rows, chans), F32),
            pltpu.VMEM((rows, chans), BF16),
            pltpu.VMEM((rows, chans), BF16),
        ],
        compiler_params=pltpu.CompilerParams(vmem_limit_bytes=16 << 20),
        name="backward",
    )(d, w1, xhat, slope, rstd, norm0_gain.reshape(1, chans), x3, rim, norm1)

    terms = [keep, received]
    count = 64
    for level in range(6):
        count //= 2
        step = lambda c, level=level: LEVELS[c][level][1:]
        out = sum(t[count : 2 * count] for t in terms)
        terms = [t[:count] for t in terms] + [exchange(out, step)]
        small = small + exchange(small, step)
    mine = sum(t[0] for t in terms).reshape(8, 3 * half)
    for distance in (1, 2, 4):
        bit = (x // distance) & 1
        pairs = mine.reshape(-1, 2, 3 * half)
        out = jnp.where(bit == 0, pairs[:, 1], pairs[:, 0])
        kept = jnp.where(bit == 0, pairs[:, 0], pairs[:, 1])
        step = lambda c, distance=distance: ("x", distance)
        mine = kept + exchange(out, step)
        small = small + exchange(small, step)

    mine = mine.reshape(3, half)
    out = jnp.where(core == 0, mine[2], mine[0])
    message = jnp.concatenate([small[:14].reshape(-1), out])
    other = lax.ppermute(message, "core", [(0, 1), (1, 0)])
    small_grads = small[:14] + other[: 14 * chans].reshape(14, chans)
    got = other[14 * chans :]
    conv1_grad = jnp.where(
        core == 0,
        jnp.concatenate([mine[0], got, mine[1]]),
        jnp.concatenate([mine[1], got, mine[2]]),
    )
    return (features[None], conv1_grad, small_grads)


def solution(mesh):
    torus = Mesh(mesh.devices.reshape(SHAPE), AXES)
    dp, audio = ("zh", "y"), ("zl", "x", "core")
    in_specs = (P(dp, audio), P(dp), P(), P(), P(), P(), P(), P(), P(dp, audio, None))
    out_specs = (P(dp, audio, None), P(dp + audio), P())
    return jax.shard_map(shards, mesh=torus, in_specs=in_specs, out_specs=out_specs, check_vma=False)
```

```python
import functools

import jax
import jax.numpy as jnp
import numpy as np
from jax import lax
from jax.experimental import pallas as pl
from jax.experimental.pallas import tpu as pltpu
from jax.sharding import Mesh
from jax.sharding import PartitionSpec as P

SHAPE = (2, 4, 2, 2, 2, 4, 2, 2)
AXES = ("zh", "yh", "y0", "z1", "z0", "xh", "x0", "core")
CUBE = ("y0", "z0", "x0")
CUBES = ("zh", "yh", "z1", "xh")
GROUP = 384
EPS = 1e-05
BF16, F32 = jnp.bfloat16, jnp.float32


def row_order():
    at = np.arange(GROUP).reshape(2, 2, 2, 2, 2, 2, 2, 3)
    return at.transpose(1, 3, 6, 0, 2, 4, 5, 7).reshape(1, GROUP).astype(np.int32)


def normal_cdf(v):
    return 0.5 + 0.5 * lax.erf(v * np.float32(0.5**0.5))


def normal_pdf(v):
    return jnp.exp(v * v * np.float32(-0.5)) * np.float32((2 * np.pi) ** -0.5)


def split_patches(x3_ref, rim_ref, odd_rows, even_last):
    value = x3_ref[...]
    row = lax.broadcasted_iota(jnp.int32, value.shape, 0)
    lane = lax.broadcasted_iota(jnp.int32, value.shape, 1)
    value = jnp.where(row == odd_rows - 1, value + rim_ref[0:1, :], value)
    value = jnp.where(row == even_last, value + rim_ref[1:2, :], value)
    high = value.astype(BF16).astype(F32)
    return jnp.where(lane < 20, high, value - high).astype(BF16)


def step_kernel(
    frames,
    chunk,
    meta_ref,
    order_ref,
    x3_ref,
    rim_ref,
    w3_ref,
    gain0_ref,
    shift0_ref,
    w1_ref,
    gain1_ref,
    shift1_ref,
    cot_ref,
    feat_ref,
    keep_ref,
    send_ref,
    pre0_ref,
    xhat_ref,
    slope_ref,
    rstd_ref,
    even_ref,
    patch_ref,
    pre1_ref,
    d_ref,
    dact_ref,
    dhigh_ref,
    dlow_ref,
    small_ref,
    grad_ref,
):
    chans = w1_ref.shape[1]
    half = chans // 2
    rows = x3_ref.shape[0]
    xs = split_patches(x3_ref, rim_ref, frames, 2 * frames)
    w3 = w3_ref[...]
    w3 = w3 - jnp.mean(w3, -1, keepdims=True)
    high = w3.astype(BF16).astype(F32)
    tap = lax.broadcasted_iota(jnp.int32, w3.shape, 0)
    ws = jnp.where((tap >= 10) & (tap < 20), w3 - high, high).astype(BF16)
    pre0_ref[...] = jnp.dot(xs, ws, preferred_element_type=F32)
    gain0 = jnp.broadcast_to(gain0_ref[...], (chunk, chans))
    shift0 = jnp.broadcast_to(shift0_ref[...], (chunk, chans))
    for at in range(0, rows, chunk):
        centred = pre0_ref[at : at + chunk]
        rstd = lax.rsqrt(jnp.mean(centred * centred, -1, keepdims=True) + EPS)
        xhat = centred * rstd
        v = xhat * gain0 + shift0
        cdf = normal_cdf(v)
        xhat_ref[at : at + chunk] = xhat
        slope_ref[at : at + chunk] = cdf + v * normal_pdf(v)
        rstd_ref[at : at + chunk] = jnp.broadcast_to(rstd, (chunk, 128))
        act = v * cdf
        if at < frames:
            patch_ref[at : at + chunk, chans : 2 * chans] = act.astype(BF16)
        else:
            even_ref[at - frames : at - frames + chunk] = act
    for at in range(0, frames, chunk):
        patch_ref[at : at + chunk, :chans] = even_ref[at : at + chunk].astype(BF16)
        patch_ref[at : at + chunk, 2 * chans :] = even_ref[at + 1 : at + 1 + chunk].astype(BF16)
    pre1_ref[...] = jnp.dot(patch_ref[...], w1_ref[...], preferred_element_type=F32)
    gain1 = jnp.broadcast_to(gain1_ref[...], (chunk, chans))
    shift1 = jnp.broadcast_to(shift1_ref[...], (chunk, chans))
    sum_gain = jnp.zeros((chunk, chans), F32)
    sum_shift = jnp.zeros((chunk, chans), F32)
    for at in range(0, frames, chunk):
        pre = pre1_ref[at : at + chunk]
        centred = pre - jnp.mean(pre, -1, keepdims=True)
        rstd = lax.rsqrt(jnp.mean(centred * centred, -1, keepdims=True) + EPS)
        xhat = centred * rstd
        v = xhat * gain1 + shift1
        cdf = normal_cdf(v)
        frame = at + lax.broadcasted_iota(jnp.int32, (chunk, chans), 0)
        valid = frame < meta_ref[0]
        feat_ref[at : at + chunk] = jnp.where(valid, v * cdf, 0.0).astype(BF16)
        dv = cot_ref[at : at + chunk].astype(F32) * (cdf + v * normal_pdf(v))
        dv = jnp.where(valid, dv, 0.0)
        sum_gain = sum_gain + dv * xhat
        sum_shift = sum_shift + dv
        dx = dv * gain1
        first = jnp.mean(dx, -1, keepdims=True)
        second = jnp.mean(dx * xhat, -1, keepdims=True)
        d_ref[at : at + chunk] = (rstd * (dx - first - xhat * second)).astype(BF16)
    small_ref[12:13] = jnp.sum(sum_gain, 0, keepdims=True)
    small_ref[13:14] = jnp.sum(sum_shift, 0, keepdims=True)
    small_ref[14:16] = jnp.zeros((2, chans), F32)

    source = lax.broadcasted_iota(jnp.int32, (GROUP, GROUP), 0)
    place = (source == order_ref[...]).astype(F32).astype(BF16)
    over_rows = (((0,), (0,)), ((), ()))
    part = GROUP // 8
    for group in range(3 * chans // GROUP):
        lanes = jnp.dot(patch_ref[:, group * GROUP : (group + 1) * GROUP], place, preferred_element_type=F32).astype(BF16)
        grad = lax.dot_general(lanes, d_ref[...], over_rows, preferred_element_type=F32)
        for cube in range(8):
            for side in range(2):
                grad_ref[side, cube, group * part : (group + 1) * part] = grad[
                    cube * part : (cube + 1) * part, side * half : (side + 1) * half
                ]

    def spread(tap):
        return lax.dot_general(
            d_ref[...],
            w1_ref[tap * chans : (tap + 1) * chans],
            (((1,), (1,)), ((), ())),
            preferred_element_type=F32,
        )

    dact_ref[:frames] = spread(1)
    dact_ref[frames : 2 * frames] = spread(0)
    dact_ref[2 * frames :] = jnp.zeros((rows - 2 * frames, chans), F32)
    dact_ref[frames + 1 : 2 * frames + 1] += spread(2)
    sum_gain = jnp.zeros((chunk, chans), F32)
    sum_shift = jnp.zeros((chunk, chans), F32)
    for at in range(0, rows, chunk):
        xhat = xhat_ref[at : at + chunk]
        dv = dact_ref[at : at + chunk] * slope_ref[at : at + chunk]
        sum_gain = sum_gain + dv * xhat
        sum_shift = sum_shift + dv
        dx = dv * gain0
        first = jnp.mean(dx, -1, keepdims=True)
        second = jnp.mean(dx * xhat, -1, keepdims=True)
        d = rstd_ref[at : at + chunk, :1] * (dx - first - xhat * second)
        high = d.astype(BF16)
        dhigh_ref[at : at + chunk] = high
        dlow_ref[at : at + chunk] = (d - high.astype(F32)).astype(BF16)
    by_high = lax.dot_general(xs, dhigh_ref[...], over_rows, preferred_element_type=F32)
    by_low = lax.dot_general(xs, dlow_ref[...], over_rows, preferred_element_type=F32)
    small_ref[0:10] = by_high[0:10] + by_high[20:30] + by_low[0:10]
    small_ref[10:11] = jnp.sum(sum_gain, 0, keepdims=True)
    small_ref[11:12] = jnp.sum(sum_shift, 0, keepdims=True)
    last = grad_ref.shape[2]
    for side in range(2):
        for cube in range(8):
            row = small_ref[8 * side + cube : 8 * side + cube + 1]
            grad_ref[side, cube, last - 8 : last - 7] = row[:, :half]
            grad_ref[side, cube, last - 7 : last - 6] = row[:, half:]
            grad_ref[side, cube, last - 6 :] = jnp.zeros((6, half), F32)
    core = meta_ref[1]
    keep_ref[...] = grad_ref[core]
    send_ref[...] = grad_ref[1 - core]


VMEM = pl.BlockSpec(memory_space=pltpu.VMEM)
SMEM = pl.BlockSpec(memory_space=pltpu.SMEM)


def shards(
    waveform,
    lengths,
    conv0_weight,
    norm0_gain,
    norm0_shift,
    conv1_weight,
    norm1_gain,
    norm1_shift,
    cotangent,
):
    position = lax.axis_index(("z1", "z0", "xh", "x0", "core"))
    core = lax.axis_index("core")
    samples_dev = waveform.shape[1]
    frames = samples_dev // 10
    chans = conv1_weight.shape[2]
    length = lengths[0]
    sample_pos = position * samples_dev + jnp.arange(samples_dev, dtype=jnp.int32)
    cleaned = jnp.where(sample_pos < length, waveform[0], 0.0)

    first = cleaned[:10]
    rim_odd = jnp.concatenate([jnp.zeros((5,), F32), first[:5]])
    rim = jnp.stack([jnp.tile(rim_odd, 3), jnp.tile(first, 3)])
    back = []
    for i in range(int(np.prod(SHAPE))):
        if i % 64:
            back.append((i, i - 1))
    rim = lax.ppermute(rim, AXES, back)

    odd = jnp.concatenate([cleaned[5:], jnp.zeros((5,), F32)]).reshape(frames, 10)
    even = cleaned.reshape(frames, 10)
    rows = 2 * frames + 16
    patches = jnp.concatenate([odd, even, jnp.zeros((16, 10), F32)], 0)
    x3 = jnp.concatenate([patches, patches, patches], 1)
    w3 = jnp.concatenate([conv0_weight, conv0_weight, conv0_weight], 0)

    meta = jnp.stack([length // 10 - position * frames, core]).astype(jnp.int32)
    half = chans // 2
    chunk = 16
    shape = jax.ShapeDtypeStruct
    features, keep, send = pl.pallas_call(
        functools.partial(step_kernel, frames, chunk),
        out_shape=(
            shape((frames, chans), BF16),
            shape((8, 200, half), F32),
            shape((8, 200, half), F32),
        ),
        in_specs=[SMEM] + [VMEM] * 10,
        out_specs=(VMEM,) * 3,
        scratch_shapes=[
            pltpu.VMEM((rows, chans), F32),
            pltpu.VMEM((rows, chans), F32),
            pltpu.VMEM((rows, chans), F32),
            pltpu.VMEM((rows, 128), F32),
            pltpu.VMEM((rows - frames, chans), F32),
            pltpu.VMEM((frames, 3 * chans), BF16),
            pltpu.VMEM((frames, chans), F32),
            pltpu.VMEM((frames, chans), BF16),
            pltpu.VMEM((rows, chans), F32),
            pltpu.VMEM((rows, chans), BF16),
            pltpu.VMEM((rows, chans), BF16),
            pltpu.VMEM((16, chans), F32),
            pltpu.VMEM((2, 8, 200, half), F32),
        ],
        compiler_params=pltpu.CompilerParams(vmem_limit_bytes=32 << 20),
        name="step",
    )(
        meta,
        row_order(),
        x3,
        rim,
        w3,
        norm0_gain.reshape(1, chans),
        norm0_shift.reshape(1, chans),
        conv1_weight.reshape(3 * chans, chans),
        norm1_gain.reshape(1, chans),
        norm1_shift.reshape(1, chans),
        cotangent[0],
    )
    mine = keep + lax.ppermute(send, "core", [(0, 1), (1, 0)])
    mine = jnp.sum(lax.all_to_all(mine, CUBE, 0, 0, tiled=True), 0)
    line = mine[192:194].reshape(1, chans)
    message = jnp.concatenate([mine[:192].reshape(64, 3 * half), jnp.broadcast_to(line, (64, chans))], 1)
    mine = jnp.sum(lax.all_to_all(message, CUBES, 0, 0, tiled=True), 0)
    part, line = mine[: 3 * half].reshape(3, half), mine[3 * half :]
    out = jnp.where(core == 0, part[2], part[0])
    message = jnp.broadcast_to(jnp.concatenate([line, out])[None], (16, chans + half))
    gathered = lax.all_to_all(message, ("core",) + CUBE, 0, 0, tiled=True)
    small_grads = gathered[:14, :chans]
    peer = (1 - core) * 8 + lax.axis_index(CUBE)
    got = lax.dynamic_slice(gathered, (peer, chans), (1, half))[0]
    conv1_grad = jnp.where(
        core == 0,
        jnp.concatenate([part[0], got, part[1]]),
        jnp.concatenate([part[1], got, part[2]]),
    )
    return (features[None], conv1_grad, small_grads)


def solution(mesh):
    torus = Mesh(mesh.devices.reshape(SHAPE), AXES)
    dp, audio = AXES[:3], AXES[3:]
    in_specs = (P(dp, audio), P(dp), P(), P(), P(), P(), P(), P(), P(dp, audio, None))
    out_specs = (P(dp, audio, None), P(dp + audio), P())
    return jax.shard_map(shards, mesh=torus, in_specs=in_specs, out_specs=out_specs, check_vma=False)
```

```python
import functools

import jax
import jax.numpy as jnp
import numpy as np
from jax import lax
from jax.experimental import pallas as pl
from jax.experimental.pallas import tpu as pltpu
from jax.sharding import Mesh
from jax.sharding import PartitionSpec as P

SHAPE = (2, 4, 2, 2, 2, 4, 2, 2)
AXES = ("zh", "yh", "y0", "z1", "z0", "xh", "x0", "core")
CUBE = ("y0", "z0", "x0")
CUBES = ("zh", "yh", "z1", "xh")
GROUP = 384
EPS = 1e-05
BF16, F32 = jnp.bfloat16, jnp.float32


def row_order(place):
    chunk = (place * 171) >> 9
    row = place - 3 * chunk
    for source, target in ((6, 5), (5, 3), (4, 0), (3, 6), (2, 4), (1, 2), (0, 1)):
        row = row + (((chunk >> source) & 1) << target) * 3
    return row


def normal_cdf(v):
    return 0.5 + 0.5 * lax.erf(v * np.float32(0.5**0.5))


def normal_pdf(v):
    return jnp.exp(v * v * np.float32(-0.5)) * np.float32((2 * np.pi) ** -0.5)


def split_patches(x3_ref, rim_ref, odd_rows, even_last):
    value = x3_ref[...]
    row = lax.broadcasted_iota(jnp.int32, value.shape, 0)
    lane = lax.broadcasted_iota(jnp.int32, value.shape, 1)
    value = jnp.where(row == odd_rows - 1, value + rim_ref[0:1, :], value)
    value = jnp.where(row == even_last, value + rim_ref[1:2, :], value)
    high = value.astype(BF16).astype(F32)
    return jnp.where(lane < 20, high, value - high).astype(BF16)


def step_kernel(
    frames,
    chunk,
    meta_ref,
    x3_ref,
    rim_ref,
    w0_hbm,
    gain0_hbm,
    shift0_hbm,
    w1_hbm,
    gain1_hbm,
    shift1_hbm,
    cot_hbm,
    feat_ref,
    keep_ref,
    send_ref,
    pre0_ref,
    xhat_ref,
    slope_ref,
    rstd_ref,
    even_ref,
    patch_ref,
    pre1_ref,
    d_ref,
    dact_ref,
    dhigh_ref,
    dlow_ref,
    small_ref,
    grad_ref,
    taps_ref,
    w0_ref,
    gain0_ref,
    shift0_ref,
    w1_ref,
    gain1_ref,
    shift1_ref,
    cot_ref,
    sems,
):
    arriving = []
    sources = (w0_hbm, gain0_hbm, shift0_hbm, w1_hbm, gain1_hbm, shift1_hbm, cot_hbm)
    targets = (w0_ref, gain0_ref, shift0_ref, w1_ref, gain1_ref, shift1_ref, cot_ref)
    for i, (source, target) in enumerate(zip(sources, targets)):
        arriving.append(pltpu.make_async_copy(source, target, sems.at[i]))
        arriving[-1].start()
    chans = w1_ref.shape[1]
    half = chans // 2
    rows = x3_ref.shape[0]
    xs = split_patches(x3_ref, rim_ref, frames, 2 * frames)
    arriving[0].wait()
    w0 = w0_ref[...]
    w0 = w0 - jnp.mean(w0, -1, keepdims=True)
    high = w0.astype(BF16).astype(F32)
    taps_ref[0:10] = high
    taps_ref[10:20] = w0 - high
    taps_ref[20:30] = high
    ws = taps_ref[0:30].astype(BF16)
    pre0_ref[...] = jnp.dot(xs, ws, preferred_element_type=F32)
    arriving[1].wait()
    arriving[2].wait()
    gain0 = jnp.broadcast_to(gain0_ref[...], (chunk, chans))
    shift0 = jnp.broadcast_to(shift0_ref[...], (chunk, chans))
    for at in range(0, rows, chunk):
        centred = pre0_ref[at : at + chunk]
        rstd = lax.rsqrt(jnp.mean(centred * centred, -1, keepdims=True) + EPS)
        xhat = centred * rstd
        v = xhat * gain0 + shift0
        cdf = normal_cdf(v)
        xhat_ref[at : at + chunk] = xhat
        slope_ref[at : at + chunk] = cdf + v * normal_pdf(v)
        rstd_ref[at : at + chunk] = jnp.broadcast_to(rstd, (chunk, 128))
        act = v * cdf
        if at < frames:
            patch_ref[at : at + chunk, chans : 2 * chans] = act.astype(BF16)
        else:
            even_ref[at - frames : at - frames + chunk] = act
    for at in range(0, frames, chunk):
        patch_ref[at : at + chunk, :chans] = even_ref[at : at + chunk].astype(BF16)
        patch_ref[at : at + chunk, 2 * chans :] = even_ref[at + 1 : at + 1 + chunk].astype(BF16)
    arriving[3].wait()
    pre1_ref[...] = jnp.dot(patch_ref[...], w1_ref[...], preferred_element_type=F32)
    for copy in arriving[4:]:
        copy.wait()
    gain1 = jnp.broadcast_to(gain1_ref[...], (chunk, chans))
    shift1 = jnp.broadcast_to(shift1_ref[...], (chunk, chans))
    sum_gain = jnp.zeros((chunk, chans), F32)
    sum_shift = jnp.zeros((chunk, chans), F32)
    for at in range(0, frames, chunk):
        pre = pre1_ref[at : at + chunk]
        centred = pre - jnp.mean(pre, -1, keepdims=True)
        rstd = lax.rsqrt(jnp.mean(centred * centred, -1, keepdims=True) + EPS)
        xhat = centred * rstd
        v = xhat * gain1 + shift1
        cdf = normal_cdf(v)
        frame = at + lax.broadcasted_iota(jnp.int32, (chunk, chans), 0)
        valid = frame < meta_ref[0]
        feat_ref[at : at + chunk] = jnp.where(valid, v * cdf, 0.0).astype(BF16)
        dv = cot_ref[at : at + chunk].astype(F32) * (cdf + v * normal_pdf(v))
        dv = jnp.where(valid, dv, 0.0)
        sum_gain = sum_gain + dv * xhat
        sum_shift = sum_shift + dv
        dx = dv * gain1
        first = jnp.mean(dx, -1, keepdims=True)
        second = jnp.mean(dx * xhat, -1, keepdims=True)
        d_ref[at : at + chunk] = (rstd * (dx - first - xhat * second)).astype(BF16)
    small_ref[12:13] = jnp.sum(sum_gain, 0, keepdims=True)
    small_ref[13:14] = jnp.sum(sum_shift, 0, keepdims=True)
    small_ref[14:16] = jnp.zeros((2, chans), F32)

    source = lax.broadcasted_iota(jnp.int32, (GROUP, GROUP), 0)
    order = row_order(lax.broadcasted_iota(jnp.int32, (1, GROUP), 1))
    place = (source == order).astype(F32).astype(BF16)
    over_rows = (((0,), (0,)), ((), ()))
    part = GROUP // 8
    for group in range(3 * chans // GROUP):
        lanes = jnp.dot(patch_ref[:, group * GROUP : (group + 1) * GROUP], place, preferred_element_type=F32).astype(BF16)
        grad = lax.dot_general(lanes, d_ref[...], over_rows, preferred_element_type=F32)
        for cube in range(8):
            for side in range(2):
                grad_ref[side, cube, group * part : (group + 1) * part] = grad[
                    cube * part : (cube + 1) * part, side * half : (side + 1) * half
                ]

    def spread(tap):
        return lax.dot_general(
            d_ref[...],
            w1_ref[tap * chans : (tap + 1) * chans],
            (((1,), (1,)), ((), ())),
            preferred_element_type=F32,
        )

    dact_ref[:frames] = spread(1)
    dact_ref[frames : 2 * frames] = spread(0)
    dact_ref[2 * frames :] = jnp.zeros((rows - 2 * frames, chans), F32)
    dact_ref[frames + 1 : 2 * frames + 1] += spread(2)
    sum_gain = jnp.zeros((chunk, chans), F32)
    sum_shift = jnp.zeros((chunk, chans), F32)
    for at in range(0, rows, chunk):
        xhat = xhat_ref[at : at + chunk]
        dv = dact_ref[at : at + chunk] * slope_ref[at : at + chunk]
        sum_gain = sum_gain + dv * xhat
        sum_shift = sum_shift + dv
        dx = dv * gain0
        first = jnp.mean(dx, -1, keepdims=True)
        second = jnp.mean(dx * xhat, -1, keepdims=True)
        d = rstd_ref[at : at + chunk, :1] * (dx - first - xhat * second)
        high = d.astype(BF16)
        dhigh_ref[at : at + chunk] = high
        dlow_ref[at : at + chunk] = (d - high.astype(F32)).astype(BF16)
    by_high = lax.dot_general(xs, dhigh_ref[...], over_rows, preferred_element_type=F32)
    by_low = lax.dot_general(xs, dlow_ref[...], over_rows, preferred_element_type=F32)
    small_ref[0:10] = by_high[0:10] + by_high[20:30] + by_low[0:10]
    small_ref[10:11] = jnp.sum(sum_gain, 0, keepdims=True)
    small_ref[11:12] = jnp.sum(sum_shift, 0, keepdims=True)
    last = grad_ref.shape[2]
    for side in range(2):
        for cube in range(8):
            row = small_ref[8 * side + cube : 8 * side + cube + 1]
            grad_ref[side, cube, last - 8 : last - 7] = row[:, :half]
            grad_ref[side, cube, last - 7 : last - 6] = row[:, half:]
            grad_ref[side, cube, last - 6 :] = jnp.zeros((6, half), F32)
    core = meta_ref[1]
    keep_ref[...] = grad_ref[core]
    send_ref[...] = grad_ref[1 - core]


HBM = pl.BlockSpec(memory_space=pltpu.HBM)
VMEM = pl.BlockSpec(memory_space=pltpu.VMEM)
SMEM = pl.BlockSpec(memory_space=pltpu.SMEM)


def shards(
    waveform,
    lengths,
    conv0_weight,
    norm0_gain,
    norm0_shift,
    conv1_weight,
    norm1_gain,
    norm1_shift,
    cotangent,
):
    position = lax.axis_index(("z1", "z0", "xh", "x0", "core"))
    core = lax.axis_index("core")
    samples_dev = waveform.shape[1]
    frames = samples_dev // 10
    chans = conv1_weight.shape[2]
    length = lengths[0]
    start = position * samples_dev
    sample_pos = start + lax.broadcasted_iota(jnp.int32, (1, samples_dev), 1)

    lane = lax.broadcasted_iota(jnp.int32, (1, 10), 1)
    first = jnp.where(start + lane < length, waveform[:, :10], 0.0)
    rim_odd = jnp.pad(first[:, :5], ((0, 0), (5, 0)))
    rim = jnp.concatenate([jnp.tile(rim_odd, (1, 3)), jnp.tile(first, (1, 3))], 0)
    back = []
    for i in range(int(np.prod(SHAPE))):
        if i % 64:
            back.append((i, i - 1))
    rim = lax.ppermute(rim, AXES, back)

    cleaned = jnp.where(sample_pos < length, waveform, 0.0)[0]
    odd = jnp.concatenate([cleaned[5:], jnp.zeros((5,), F32)]).reshape(frames, 10)
    even = cleaned.reshape(frames, 10)
    rows = 2 * frames + 16
    patches = jnp.concatenate([odd, even, jnp.zeros((16, 10), F32)], 0)
    x3 = jnp.concatenate([patches, patches, patches], 1)
    meta = jnp.stack([length // 10 - position * frames, core]).astype(jnp.int32)
    half = chans // 2
    chunk = 16
    shape = jax.ShapeDtypeStruct
    features, keep, send = pl.pallas_call(
        functools.partial(step_kernel, frames, chunk),
        out_shape=(
            shape((frames, chans), BF16),
            shape((8, 200, half), F32),
            shape((8, 200, half), F32),
        ),
        in_specs=[SMEM] + [VMEM] * 2 + [HBM] * 7,
        out_specs=(VMEM,) * 3,
        scratch_shapes=[
            pltpu.VMEM((rows, chans), F32),
            pltpu.VMEM((rows, chans), F32),
            pltpu.VMEM((rows, chans), F32),
            pltpu.VMEM((rows, 128), F32),
            pltpu.VMEM((rows - frames, chans), F32),
            pltpu.VMEM((frames, 3 * chans), BF16),
            pltpu.VMEM((frames, chans), F32),
            pltpu.VMEM((frames, chans), BF16),
            pltpu.VMEM((rows, chans), F32),
            pltpu.VMEM((rows, chans), BF16),
            pltpu.VMEM((rows, chans), BF16),
            pltpu.VMEM((16, chans), F32),
            pltpu.VMEM((2, 8, 200, half), F32),
            pltpu.VMEM((32, chans), F32),
            pltpu.VMEM((10, chans), F32),
            pltpu.VMEM((1, chans), F32),
            pltpu.VMEM((1, chans), F32),
            pltpu.VMEM((3 * chans, chans), BF16),
            pltpu.VMEM((1, chans), F32),
            pltpu.VMEM((1, chans), F32),
            pltpu.VMEM((frames, chans), BF16),
            pltpu.SemaphoreType.DMA((7,)),
        ],
        compiler_params=pltpu.CompilerParams(vmem_limit_bytes=32 << 20),
        name="step",
    )(
        meta,
        x3,
        rim,
        *(
            pltpu.with_memory_space_constraint(operand, pltpu.HBM)
            for operand in (
                conv0_weight,
                norm0_gain.reshape(1, chans),
                norm0_shift.reshape(1, chans),
                conv1_weight.reshape(3 * chans, chans),
                norm1_gain.reshape(1, chans),
                norm1_shift.reshape(1, chans),
                cotangent[0],
            )
        ),
    )
    send, first_core = lax.optimization_barrier((send, core == 0))
    mine = keep + lax.ppermute(send, "core", [(0, 1), (1, 0)])
    mine = jnp.sum(lax.all_to_all(mine, CUBE, 0, 0, tiled=True), 0)
    line = mine[192:194].reshape(1, chans)
    message = jnp.concatenate([mine[:192].reshape(64, 3 * half), jnp.broadcast_to(line, (64, chans))], 1)
    mine = jnp.sum(lax.all_to_all(message, CUBES, 0, 0, tiled=True), 0)
    part, line = mine[: 3 * half].reshape(3, half), mine[3 * half :]
    out = jnp.where(first_core, part[2], part[0])
    message = jnp.broadcast_to(jnp.concatenate([line, out])[None], (16, chans + half))
    gathered = lax.all_to_all(message, ("core",) + CUBE, 0, 0, tiled=True)
    small_grads = gathered[:14, :chans]
    peer = (1 - core) * 8 + lax.axis_index(CUBE)
    got = lax.dynamic_slice(gathered, (peer, chans), (1, half))[0]
    conv1_grad = jnp.where(
        first_core,
        jnp.concatenate([part[0], got, part[1]]),
        jnp.concatenate([part[1], got, part[2]]),
    )
    return (features[None], conv1_grad, small_grads)


def solution(mesh):
    torus = Mesh(mesh.devices.reshape(SHAPE), AXES)
    dp, audio = AXES[:3], AXES[3:]
    in_specs = (P(dp, audio), P(dp), P(), P(), P(), P(), P(), P(), P(dp, audio, None))
    out_specs = (P(dp, audio, None), P(dp + audio), P())
    return jax.shard_map(shards, mesh=torus, in_specs=in_specs, out_specs=out_specs, check_vma=False)
```

```python
import functools

import jax
import jax.numpy as jnp
import numpy as np
from jax import lax
from jax.experimental import pallas as pl
from jax.experimental.pallas import tpu as pltpu
from jax.sharding import Mesh
from jax.sharding import PartitionSpec as P

SHAPE = (2, 4, 2, 2, 2, 4, 2, 2)
AXES = ("zh", "yh", "y0", "z1", "z0", "xh", "x0", "core")
CUBE = ("y0", "z0", "x0")
CUBES = ("zh", "yh", "z1", "xh")
GROUP = 384
EPS = 1e-05
BF16, F32 = jnp.bfloat16, jnp.float32


def cubes():
    groups = {}
    for i in range(int(np.prod(SHAPE))):
        zh, yh, y0, z1, z0, xh, x0, core = (int(v) for v in np.unravel_index(i, SHAPE))
        z, y, x = zh * 4 + z1 * 2 + z0, yh * 2 + y0, xh * 2 + x0
        cube = tuple(((v - core) % 8) // 2 for v in (z, y, x)) + (core,)
        groups.setdefault(cube, [0] * 8)[(y0 * 2 + z0) * 2 + x0] = i
    return list(groups.values())


def row_order(place):
    chunk = (place * 171) >> 9
    row = place - 3 * chunk
    for source, target in ((6, 5), (5, 3), (4, 0), (3, 6), (2, 4), (1, 2), (0, 1)):
        row = row + (((chunk >> source) & 1) << target) * 3
    return row


def normal_cdf(v):
    return 0.5 + 0.5 * lax.erf(v * np.float32(0.5**0.5))


def normal_pdf(v):
    return jnp.exp(v * v * np.float32(-0.5)) * np.float32((2 * np.pi) ** -0.5)


def split_patches(x3_ref, rim_ref, odd_last, even_last):
    value = x3_ref[...]
    width = value.shape[1]
    rim = jnp.broadcast_to(rim_ref[...], (8, 128))
    five = jnp.where(lax.broadcasted_iota(jnp.int32, rim.shape, 1) < 5, rim, 0.0)
    even = rim + pltpu.roll(rim, 10, 1) + pltpu.roll(rim, 20, 1)
    odd = pltpu.roll(five, 5, 1) + pltpu.roll(five, 15, 1) + pltpu.roll(five, 25, 1)
    row = lax.broadcasted_iota(jnp.int32, value.shape, 0)
    lane = lax.broadcasted_iota(jnp.int32, value.shape, 1)
    value = jnp.where(row == odd_last, value + odd[0:1, :width], value)
    value = jnp.where(row == even_last, value + even[0:1, :width], value)
    high = value.astype(BF16).astype(F32)
    return jnp.where(lane < 20, high, value - high).astype(BF16)


def step_kernel(
    frames,
    chunk,
    meta_ref,
    x3_ref,
    rim_ref,
    w0_hbm,
    gain0_hbm,
    shift0_hbm,
    w1_hbm,
    gain1_hbm,
    shift1_hbm,
    cot_hbm,
    feat_ref,
    keep_ref,
    send_ref,
    pre0_ref,
    xhat_ref,
    slope_ref,
    rstd_ref,
    even_ref,
    patch_ref,
    pre1_ref,
    d_ref,
    dact_ref,
    dhigh_ref,
    dlow_ref,
    small_ref,
    sides_ref,
    taps_ref,
    w0_ref,
    gain0_ref,
    shift0_ref,
    w1_ref,
    gain1_ref,
    shift1_ref,
    cot_ref,
    sems,
):
    arriving = []
    sources = (w0_hbm, gain0_hbm, shift0_hbm, w1_hbm, gain1_hbm, shift1_hbm, cot_hbm)
    targets = (w0_ref, gain0_ref, shift0_ref, w1_ref, gain1_ref, shift1_ref, cot_ref)
    for i, (source, target) in enumerate(zip(sources, targets)):
        arriving.append(pltpu.make_async_copy(source, target, sems.at[i]))
        arriving[-1].start()
    chans = w1_ref.shape[1]
    half = chans // 2
    rows = x3_ref.shape[0]
    core = meta_ref[1]
    xs = split_patches(x3_ref, rim_ref, frames - 1, 2 * frames)
    arriving[0].wait()
    w0 = w0_ref[...]
    w0 = w0 - jnp.mean(w0, -1, keepdims=True)
    high = w0.astype(BF16).astype(F32)
    taps_ref[0:10] = high
    taps_ref[10:20] = w0 - high
    taps_ref[20:30] = high
    ws = taps_ref[0:30].astype(BF16)
    pre0_ref[...] = jnp.dot(xs, ws, preferred_element_type=F32)
    arriving[1].wait()
    arriving[2].wait()
    gain0 = jnp.broadcast_to(gain0_ref[...], (chunk, chans))
    shift0 = jnp.broadcast_to(shift0_ref[...], (chunk, chans))
    for at in range(0, rows, chunk):
        centred = pre0_ref[at : at + chunk]
        rstd = lax.rsqrt(jnp.mean(centred * centred, -1, keepdims=True) + EPS)
        xhat = centred * rstd
        v = xhat * gain0 + shift0
        cdf = normal_cdf(v)
        xhat_ref[at : at + chunk] = xhat
        slope_ref[at : at + chunk] = cdf + v * normal_pdf(v)
        rstd_ref[at : at + chunk] = jnp.broadcast_to(rstd, (chunk, 128))
        act = v * cdf
        if at < frames:
            patch_ref[at : at + chunk, chans : 2 * chans] = act.astype(BF16)
        else:
            even_ref[at - frames : at - frames + chunk] = act
    for at in range(0, frames, chunk):
        patch_ref[at : at + chunk, :chans] = even_ref[at : at + chunk].astype(BF16)
        patch_ref[at : at + chunk, 2 * chans :] = even_ref[at + 1 : at + 1 + chunk].astype(BF16)
    arriving[3].wait()
    pre1_ref[...] = jnp.dot(patch_ref[...], w1_ref[...], preferred_element_type=F32)
    for copy in arriving[4:]:
        copy.wait()
    gain1 = jnp.broadcast_to(gain1_ref[...], (chunk, chans))
    shift1 = jnp.broadcast_to(shift1_ref[...], (chunk, chans))
    sum_gain = jnp.zeros((chunk, chans), F32)
    sum_shift = jnp.zeros((chunk, chans), F32)
    for at in range(0, frames, chunk):
        pre = pre1_ref[at : at + chunk]
        centred = pre - jnp.mean(pre, -1, keepdims=True)
        rstd = lax.rsqrt(jnp.mean(centred * centred, -1, keepdims=True) + EPS)
        xhat = centred * rstd
        v = xhat * gain1 + shift1
        cdf = normal_cdf(v)
        frame = at + lax.broadcasted_iota(jnp.int32, (chunk, chans), 0)
        valid = frame < meta_ref[0]
        feat_ref[at : at + chunk] = jnp.where(valid, v * cdf, 0.0).astype(BF16)
        dv = cot_ref[at : at + chunk].astype(F32) * (cdf + v * normal_pdf(v))
        dv = jnp.where(valid, dv, 0.0)
        sum_gain = sum_gain + dv * xhat
        sum_shift = sum_shift + dv
        dx = dv * gain1
        first = jnp.mean(dx, -1, keepdims=True)
        second = jnp.mean(dx * xhat, -1, keepdims=True)
        d = rstd * (dx - first - xhat * second)
        d_ref[at : at + chunk] = d.astype(BF16)
        left, right = d[:, :half], d[:, half:]
        sides_ref[at : at + chunk, :half] = jnp.where(core == 0, right, left).astype(BF16)
        sides_ref[at : at + chunk, half:] = jnp.where(core == 0, left, right).astype(BF16)
    small_ref[12:13] = jnp.sum(sum_gain, 0, keepdims=True)
    small_ref[13:14] = jnp.sum(sum_shift, 0, keepdims=True)
    small_ref[14:16] = jnp.zeros((2, chans), F32)

    source = lax.broadcasted_iota(jnp.int32, (GROUP, GROUP), 0)
    order = row_order(lax.broadcasted_iota(jnp.int32, (1, GROUP), 1))
    place = (source == order).astype(F32).astype(BF16)
    over_rows = (((0,), (0,)), ((), ()))
    part = GROUP // 8
    for group in range(3 * chans // GROUP):
        lanes = jnp.dot(patch_ref[:, group * GROUP : (group + 1) * GROUP], place, preferred_element_type=F32).astype(BF16)
        grad = lax.dot_general(lanes, sides_ref[...], over_rows, preferred_element_type=F32)
        for cube in range(8):
            block = grad[cube * part : (cube + 1) * part]
            send_ref[cube, group * part : (group + 1) * part] = block[:, :half]
            keep_ref[cube, group * part : (group + 1) * part] = block[:, half:]

    def spread(tap):
        return lax.dot_general(
            d_ref[...],
            w1_ref[tap * chans : (tap + 1) * chans],
            (((1,), (1,)), ((), ())),
            preferred_element_type=F32,
        )

    dact_ref[:frames] = spread(1)
    dact_ref[frames : 2 * frames] = spread(0)
    dact_ref[2 * frames :] = jnp.zeros((rows - 2 * frames, chans), F32)
    dact_ref[frames + 1 : 2 * frames + 1] += spread(2)
    sum_gain = jnp.zeros((chunk, chans), F32)
    sum_shift = jnp.zeros((chunk, chans), F32)
    for at in range(0, rows, chunk):
        xhat = xhat_ref[at : at + chunk]
        dv = dact_ref[at : at + chunk] * slope_ref[at : at + chunk]
        sum_gain = sum_gain + dv * xhat
        sum_shift = sum_shift + dv
        dx = dv * gain0
        first = jnp.mean(dx, -1, keepdims=True)
        second = jnp.mean(dx * xhat, -1, keepdims=True)
        d = rstd_ref[at : at + chunk, :1] * (dx - first - xhat * second)
        high = d.astype(BF16)
        dhigh_ref[at : at + chunk] = high
        dlow_ref[at : at + chunk] = (d - high.astype(F32)).astype(BF16)
    by_high = lax.dot_general(xs, dhigh_ref[...], over_rows, preferred_element_type=F32)
    by_low = lax.dot_general(xs, dlow_ref[...], over_rows, preferred_element_type=F32)
    small_ref[0:10] = by_high[0:10] + by_high[20:30] + by_low[0:10]
    small_ref[10:11] = jnp.sum(sum_gain, 0, keepdims=True)
    small_ref[11:12] = jnp.sum(sum_shift, 0, keepdims=True)
    last = keep_ref.shape[1] - 8
    for out_ref, owner in ((keep_ref, core), (send_ref, 1 - core)):
        for cube in range(8):
            row = small_ref[pl.ds(8 * owner + cube, 1)]
            out_ref[cube, last : last + 1] = row[:, :half]
            out_ref[cube, last + 1 : last + 2] = row[:, half:]
            out_ref[cube, last + 2 :] = jnp.zeros((6, half), F32)


HBM = pl.BlockSpec(memory_space=pltpu.HBM)
VMEM = pl.BlockSpec(memory_space=pltpu.VMEM)
SMEM = pl.BlockSpec(memory_space=pltpu.SMEM)


def shards(
    waveform,
    lengths,
    conv0_weight,
    norm0_gain,
    norm0_shift,
    conv1_weight,
    norm1_gain,
    norm1_shift,
    cotangent,
):
    position = lax.axis_index(("z1", "z0", "xh", "x0", "core"))
    core = lax.axis_index("core")
    samples_dev = waveform.shape[1]
    frames = samples_dev // 10
    chans = conv1_weight.shape[2]
    length = lengths[0]
    start = position * samples_dev
    sample_pos = start + lax.broadcasted_iota(jnp.int32, (1, samples_dev), 1)

    lane = lax.broadcasted_iota(jnp.int32, (1, 128), 1)
    rim = jnp.where((lane < 10) & (start + lane < length), waveform[:, :128], 0.0)
    back = []
    for i in range(int(np.prod(SHAPE))):
        if i % 64:
            back.append((i, i - 1))
    rim = lax.ppermute(rim, AXES, back)

    cleaned = jnp.where(sample_pos < length, waveform, 0.0)[0]
    odd = jnp.concatenate([cleaned[5:], jnp.zeros((5,), F32)]).reshape(frames, 10)
    even = cleaned.reshape(frames, 10)
    rows = 2 * frames + 16
    patches = jnp.concatenate([odd, even, jnp.zeros((16, 10), F32)], 0)
    x3 = jnp.concatenate([patches, patches, patches], 1)
    meta = jnp.stack([length // 10 - position * frames, core]).astype(jnp.int32)
    half = chans // 2
    chunk = 16
    shape = jax.ShapeDtypeStruct
    features, keep, send = pl.pallas_call(
        functools.partial(step_kernel, frames, chunk),
        out_shape=(
            shape((frames, chans), BF16),
            shape((8, 200, half), F32),
            shape((8, 200, half), F32),
        ),
        in_specs=[SMEM] + [VMEM] * 2 + [HBM] * 7,
        out_specs=(VMEM,) * 3,
        scratch_shapes=[
            pltpu.VMEM((rows, chans), F32),
            pltpu.VMEM((rows, chans), F32),
            pltpu.VMEM((rows, chans), F32),
            pltpu.VMEM((rows, 128), F32),
            pltpu.VMEM((rows - frames, chans), F32),
            pltpu.VMEM((frames, 3 * chans), BF16),
            pltpu.VMEM((frames, chans), F32),
            pltpu.VMEM((frames, chans), BF16),
            pltpu.VMEM((rows, chans), F32),
            pltpu.VMEM((rows, chans), BF16),
            pltpu.VMEM((rows, chans), BF16),
            pltpu.VMEM((16, chans), F32),
            pltpu.VMEM((frames, chans), BF16),
            pltpu.VMEM((32, chans), F32),
            pltpu.VMEM((10, chans), F32),
            pltpu.VMEM((1, chans), F32),
            pltpu.VMEM((1, chans), F32),
            pltpu.VMEM((3 * chans, chans), BF16),
            pltpu.VMEM((1, chans), F32),
            pltpu.VMEM((1, chans), F32),
            pltpu.VMEM((frames, chans), BF16),
            pltpu.SemaphoreType.DMA((7,)),
        ],
        compiler_params=pltpu.CompilerParams(vmem_limit_bytes=32 << 20),
        name="step",
    )(
        meta,
        x3,
        rim,
        *(
            pltpu.with_memory_space_constraint(operand, pltpu.HBM)
            for operand in (
                conv0_weight,
                norm0_gain.reshape(1, chans),
                norm0_shift.reshape(1, chans),
                conv1_weight.reshape(3 * chans, chans),
                norm1_gain.reshape(1, chans),
                norm1_shift.reshape(1, chans),
                cotangent[0],
            )
        ),
    )
    send, first_core = lax.optimization_barrier((send, core == 0))
    mine = keep + lax.ppermute(send, "core", [(0, 1), (1, 0)])
    mine = jnp.sum(lax.all_to_all(mine, AXES, 0, 0, axis_index_groups=cubes(), tiled=True), 0)
    line = mine[192:194].reshape(1, chans)
    message = jnp.concatenate([mine[:192].reshape(64, 3 * half), jnp.broadcast_to(line, (64, chans))], 1)
    mine = jnp.sum(lax.all_to_all(message, CUBES, 0, 0, tiled=True), 0)
    part, line = mine[: 3 * half].reshape(3, half), mine[3 * half :]
    out = jnp.where(first_core, part[2], part[0])
    message = jnp.broadcast_to(jnp.concatenate([line, out])[None], (16, chans + half))
    gathered = lax.all_to_all(message, ("core",) + CUBE, 0, 0, tiled=True)
    small_grads = gathered[:14, :chans]
    peer = (1 - core) * 8 + lax.axis_index(CUBE)
    got = lax.dynamic_slice(gathered, (peer, chans), (1, half))[0]
    conv1_grad = jnp.where(
        first_core,
        jnp.concatenate([part[0], got, part[1]]),
        jnp.concatenate([part[1], got, part[2]]),
    )
    return (features[None], conv1_grad, small_grads)


def solution(mesh):
    torus = Mesh(mesh.devices.reshape(SHAPE), AXES)
    dp, audio = AXES[:3], AXES[3:]
    in_specs = (P(dp, audio), P(dp), P(), P(), P(), P(), P(), P(), P(dp, audio, None))
    out_specs = (P(dp, audio, None), P(dp + audio), P())
    return jax.shard_map(shards, mesh=torus, in_specs=in_specs, out_specs=out_specs, check_vma=False)
```

```python
import functools

import jax
import jax.numpy as jnp
import numpy as np
from jax import lax
from jax.experimental import pallas as pl
from jax.experimental.pallas import tpu as pltpu
from jax.sharding import Mesh
from jax.sharding import PartitionSpec as P

SHAPE = (2,) * 10
AXES = ("z2", "y2", "y1", "y0", "z1", "z0", "x2", "x1", "x0", "core")
DP, AUDIO = AXES[:4], AXES[4:]
CUBE = ("y0", "z0", "x0")
FAR = ("z2", "y2", "x2")
GROUP = 384
EPS = 1e-05
BF16, F32 = jnp.bfloat16, jnp.float32


def cubes(bit):
    groups = {}
    for i in range(2 ** len(AXES)):
        at = dict(zip(AXES, (int(v) for v in np.unravel_index(i, SHAPE))))
        group, member = [at["core"]], 0
        for axis in "yzx":
            place = sum(at[f"{axis}{n}"] << n for n in range(3))
            moved = (place - (at["core"] << bit)) % 8
            group.append(moved & ~(1 << bit))
            member = member * 2 + ((place >> bit) & 1)
        groups.setdefault(tuple(group), [0] * 8)[member] = i
    return list(groups.values())


def row_order(place):
    chunk = (place * 171) >> 9
    row = place - 3 * chunk
    for source, target in ((6, 5), (5, 3), (4, 0), (3, 6), (2, 4), (1, 1), (0, 2)):
        row = row + (((chunk >> source) & 1) << target) * 3
    return row


def normal_cdf(v):
    return 0.5 + 0.5 * lax.erf(v * np.float32(0.5**0.5))


def normal_pdf(v):
    return jnp.exp(v * v * np.float32(-0.5)) * np.float32((2 * np.pi) ** -0.5)


def fill_patches(block_ref, rim_ref, ext_ref, xs_ref, start, length):
    frames = block_ref.shape[0]
    row = lax.broadcasted_iota(jnp.int32, (frames, 10), 0)
    lane = lax.broadcasted_iota(jnp.int32, (frames, 10), 1)
    ext_ref[...] = jnp.zeros_like(ext_ref)
    ext_ref[0:frames, 0:10] = jnp.where(start + row * 10 + lane < length, block_ref[...], 0.0)
    lane = lax.broadcasted_iota(jnp.int32, (1, 128), 1)
    rim = jnp.where((lane < 10) & (start + frames * 10 + lane < length), rim_ref[:, :128], 0.0)
    ext_ref[frames : frames + 1] = rim
    here, after = ext_ref[...], ext_ref[1 : frames + 1]
    lane = lax.broadcasted_iota(jnp.int32, (frames, 128), 1)
    later = jnp.where(lane < 5, after, 0.0)
    odd = pltpu.roll(jnp.where(lane >= 5, here[:frames], 0.0), 123, 1) + pltpu.roll(later, 5, 1)
    for at, value in ((0, odd), (frames, here)):
        value = value + pltpu.roll(value, 10, 1) + pltpu.roll(value, 20, 1)
        high = value.astype(BF16).astype(F32)
        lane = lax.broadcasted_iota(jnp.int32, value.shape, 1)
        xs_ref[at : at + value.shape[0]] = jnp.where(lane < 20, high, value - high).astype(BF16)


def step_kernel(
    frames,
    chunk,
    length_ref,
    block_ref,
    rim_ref,
    w0_hbm,
    gain0_hbm,
    shift0_hbm,
    w1_hbm,
    gain1_hbm,
    shift1_hbm,
    cot_hbm,
    feat_ref,
    keep_ref,
    send_ref,
    pre0_ref,
    xhat_ref,
    slope_ref,
    rstd_ref,
    even_ref,
    patch_ref,
    pre1_ref,
    d_ref,
    dact_ref,
    dhigh_ref,
    dlow_ref,
    small_ref,
    sides_ref,
    ext_ref,
    xs_ref,
    taps_ref,
    w0_ref,
    gain0_ref,
    shift0_ref,
    w1_ref,
    gain1_ref,
    shift1_ref,
    cot_ref,
    sems,
):
    arriving = []
    sources = (w0_hbm, gain0_hbm, shift0_hbm, w1_hbm, gain1_hbm, shift1_hbm, cot_hbm)
    targets = (w0_ref, gain0_ref, shift0_ref, w1_ref, gain1_ref, shift1_ref, cot_ref)
    for i, (source, target) in enumerate(zip(sources, targets)):
        arriving.append(pltpu.make_async_copy(source, target, sems.at[i]))
        arriving[-1].start()
    chans = w1_ref.shape[1]
    half = chans // 2
    rows = pre0_ref.shape[0]
    core = lax.axis_index("core")
    position = lax.axis_index(AUDIO)
    length = length_ref[0]
    fill_patches(block_ref, rim_ref, ext_ref, xs_ref, position * (frames * 10), length)
    xs = xs_ref[:, :30]
    arriving[0].wait()
    w0 = w0_ref[...]
    w0 = w0 - jnp.mean(w0, -1, keepdims=True)
    high = w0.astype(BF16).astype(F32)
    taps_ref[0:10] = high
    taps_ref[10:20] = w0 - high
    taps_ref[20:30] = high
    ws = taps_ref[0:30].astype(BF16)
    pre0_ref[...] = jnp.dot(xs, ws, preferred_element_type=F32)
    arriving[1].wait()
    arriving[2].wait()
    gain0 = jnp.broadcast_to(gain0_ref[...], (chunk, chans))
    shift0 = jnp.broadcast_to(shift0_ref[...], (chunk, chans))
    for at in range(0, rows, chunk):
        centred = pre0_ref[at : at + chunk]
        rstd = lax.rsqrt(jnp.mean(centred * centred, -1, keepdims=True) + EPS)
        xhat = centred * rstd
        v = xhat * gain0 + shift0
        cdf = normal_cdf(v)
        xhat_ref[at : at + chunk] = xhat
        slope_ref[at : at + chunk] = cdf + v * normal_pdf(v)
        rstd_ref[at : at + chunk] = jnp.broadcast_to(rstd, (chunk, 128))
        act = v * cdf
        if at < frames:
            patch_ref[at : at + chunk, chans : 2 * chans] = act.astype(BF16)
        else:
            even_ref[at - frames : at - frames + chunk] = act
    for at in range(0, frames, chunk):
        patch_ref[at : at + chunk, :chans] = even_ref[at : at + chunk].astype(BF16)
        patch_ref[at : at + chunk, 2 * chans :] = even_ref[at + 1 : at + 1 + chunk].astype(BF16)
    arriving[3].wait()
    pre1_ref[...] = jnp.dot(patch_ref[...], w1_ref[...], preferred_element_type=F32)
    for copy in arriving[4:]:
        copy.wait()
    gain1 = jnp.broadcast_to(gain1_ref[...], (chunk, chans))
    shift1 = jnp.broadcast_to(shift1_ref[...], (chunk, chans))
    sum_gain = jnp.zeros((chunk, chans), F32)
    sum_shift = jnp.zeros((chunk, chans), F32)
    for at in range(0, frames, chunk):
        pre = pre1_ref[at : at + chunk]
        centred = pre - jnp.mean(pre, -1, keepdims=True)
        rstd = lax.rsqrt(jnp.mean(centred * centred, -1, keepdims=True) + EPS)
        xhat = centred * rstd
        v = xhat * gain1 + shift1
        cdf = normal_cdf(v)
        frame = at + lax.broadcasted_iota(jnp.int32, (chunk, chans), 0)
        valid = (position * frames + frame) * 10 + 10 <= length
        feat_ref[at : at + chunk] = jnp.where(valid, v * cdf, 0.0).astype(BF16)
        dv = cot_ref[at : at + chunk].astype(F32) * (cdf + v * normal_pdf(v))
        dv = jnp.where(valid, dv, 0.0)
        sum_gain = sum_gain + dv * xhat
        sum_shift = sum_shift + dv
        dx = dv * gain1
        first = jnp.mean(dx, -1, keepdims=True)
        second = jnp.mean(dx * xhat, -1, keepdims=True)
        d = rstd * (dx - first - xhat * second)
        d_ref[at : at + chunk] = d.astype(BF16)
        left, right = d[:, :half], d[:, half:]
        sides_ref[at : at + chunk, :half] = jnp.where(core == 0, right, left).astype(BF16)
        sides_ref[at : at + chunk, half:] = jnp.where(core == 0, left, right).astype(BF16)
    small_ref[12:13] = jnp.sum(sum_gain, 0, keepdims=True)
    small_ref[13:14] = jnp.sum(sum_shift, 0, keepdims=True)
    small_ref[14:16] = jnp.zeros((2, chans), F32)

    source = lax.broadcasted_iota(jnp.int32, (GROUP, GROUP), 0)
    order = row_order(lax.broadcasted_iota(jnp.int32, (1, GROUP), 1))
    place = (source == order).astype(F32).astype(BF16)
    over_rows = (((0,), (0,)), ((), ()))
    part = GROUP // 8
    for group in range(3 * chans // GROUP):
        lanes = jnp.dot(patch_ref[:, group * GROUP : (group + 1) * GROUP], place, preferred_element_type=F32).astype(BF16)
        grad = lax.dot_general(lanes, sides_ref[...], over_rows, preferred_element_type=F32)
        for cube in range(8):
            block = grad[cube * part : (cube + 1) * part]
            send_ref[cube, group * part : (group + 1) * part] = block[:, :half]
            keep_ref[cube, group * part : (group + 1) * part] = block[:, half:]

    def spread(tap):
        return lax.dot_general(
            d_ref[...],
            w1_ref[tap * chans : (tap + 1) * chans],
            (((1,), (1,)), ((), ())),
            preferred_element_type=F32,
        )

    dact_ref[:frames] = spread(1)
    dact_ref[frames : 2 * frames] = spread(0)
    dact_ref[2 * frames :] = jnp.zeros((rows - 2 * frames, chans), F32)
    dact_ref[frames + 1 : 2 * frames + 1] += spread(2)
    sum_gain = jnp.zeros((chunk, chans), F32)
    sum_shift = jnp.zeros((chunk, chans), F32)
    for at in range(0, rows, chunk):
        xhat = xhat_ref[at : at + chunk]
        dv = dact_ref[at : at + chunk] * slope_ref[at : at + chunk]
        sum_gain = sum_gain + dv * xhat
        sum_shift = sum_shift + dv
        dx = dv * gain0
        first = jnp.mean(dx, -1, keepdims=True)
        second = jnp.mean(dx * xhat, -1, keepdims=True)
        d = rstd_ref[at : at + chunk, :1] * (dx - first - xhat * second)
        high = d.astype(BF16)
        dhigh_ref[at : at + chunk] = high
        dlow_ref[at : at + chunk] = (d - high.astype(F32)).astype(BF16)
    by_high = lax.dot_general(xs, dhigh_ref[...], over_rows, preferred_element_type=F32)
    by_low = lax.dot_general(xs, dlow_ref[...], over_rows, preferred_element_type=F32)
    small_ref[0:10] = by_high[0:10] + by_high[20:30] + by_low[0:10]
    small_ref[10:11] = jnp.sum(sum_gain, 0, keepdims=True)
    small_ref[11:12] = jnp.sum(sum_shift, 0, keepdims=True)
    last = keep_ref.shape[1] - 8
    for out_ref, owner in ((keep_ref, core), (send_ref, 1 - core)):
        for cube in range(8):
            row = small_ref[pl.ds(8 * owner + cube, 1)]
            out_ref[cube, last : last + 1] = row[:, :half]
            out_ref[cube, last + 1 : last + 2] = row[:, half:]
            out_ref[cube, last + 2 :] = jnp.zeros((6, half), F32)


def near_kernel(cube_ref, out_ref, sum_ref):
    sum_ref[...] = jnp.sum(cube_ref[...], 0)
    for target in range(8):
        for group in range(4):
            at = group * 48 + target * 6
            out_ref[target, group * 6 : group * 6 + 6] = sum_ref[at : at + 6]
        out_ref[target, 24:26] = sum_ref[192:194]


def far_kernel(near_ref, out_ref, sum_ref):
    sum_ref[...] = jnp.sum(near_ref[...], 0)
    for target in range(8):
        out_ref[target, 0:3] = sum_ref[target * 3 : target * 3 + 3]
        out_ref[target, 3:5] = sum_ref[24:26]


def share_kernel(far_ref, out_ref, kept_ref, sum_ref):
    sum_ref[...] = jnp.sum(far_ref[...], 0)
    first = lax.axis_index("core") == 0
    out_ref[:, 0:2] = jnp.broadcast_to(sum_ref[3:5][None], (16, 2, out_ref.shape[2]))
    other = jnp.where(first, sum_ref[2:3], sum_ref[0:1])
    out_ref[:, 2:3] = jnp.broadcast_to(other[None], (16, 1, out_ref.shape[2]))
    kept_ref[0:1] = jnp.where(first, sum_ref[0:1], sum_ref[1:2])
    kept_ref[1:2] = jnp.where(first, sum_ref[1:2], sum_ref[2:3])


def final_kernel(peer_ref, all_ref, kept_ref, grad_ref, small_ref):
    half = all_ref.shape[2]
    got = all_ref[peer_ref[0]][2:3]
    grad_ref[0:1] = kept_ref[0:1]
    grad_ref[1:2] = got
    grad_ref[2:3] = kept_ref[1:2]
    for row in range(14):
        small_ref[row : row + 1, :half] = all_ref[row, 0:1]
        small_ref[row : row + 1, half:] = all_ref[row, 1:2]


HBM = pl.BlockSpec(memory_space=pltpu.HBM)
VMEM = pl.BlockSpec(memory_space=pltpu.VMEM)
SMEM = pl.BlockSpec(memory_space=pltpu.SMEM)


def shards(
    waveform,
    lengths,
    conv0_weight,
    norm0_gain,
    norm0_shift,
    conv1_weight,
    norm1_gain,
    norm1_shift,
    cotangent,
):
    frames = waveform.shape[1] // 10
    chans = conv1_weight.shape[2]
    rows = 2 * frames + 16
    back = []
    for i in range(2 ** len(AXES)):
        if i % 2 ** len(AUDIO):
            back.append((i, i - 1))
    rim = lax.ppermute(waveform, AXES, back)
    half = chans // 2
    chunk = 16
    shape = jax.ShapeDtypeStruct
    features, keep, send = pl.pallas_call(
        functools.partial(step_kernel, frames, chunk),
        out_shape=(
            shape((frames, chans), BF16),
            shape((8, 200, half), F32),
            shape((8, 200, half), F32),
        ),
        in_specs=[SMEM] + [VMEM] * 2 + [HBM] * 7,
        out_specs=(VMEM,) * 3,
        scratch_shapes=[
            pltpu.VMEM((rows, chans), F32),
            pltpu.VMEM((rows, chans), F32),
            pltpu.VMEM((rows, chans), F32),
            pltpu.VMEM((rows, 128), F32),
            pltpu.VMEM((rows - frames, chans), F32),
            pltpu.VMEM((frames, 3 * chans), BF16),
            pltpu.VMEM((frames, chans), F32),
            pltpu.VMEM((frames, chans), BF16),
            pltpu.VMEM((rows, chans), F32),
            pltpu.VMEM((rows, chans), BF16),
            pltpu.VMEM((rows, chans), BF16),
            pltpu.VMEM((16, chans), F32),
            pltpu.VMEM((frames, chans), BF16),
            pltpu.VMEM((frames + 16, 128), F32),
            pltpu.VMEM((rows, 128), BF16),
            pltpu.VMEM((32, chans), F32),
            pltpu.VMEM((10, chans), F32),
            pltpu.VMEM((1, chans), F32),
            pltpu.VMEM((1, chans), F32),
            pltpu.VMEM((3 * chans, chans), BF16),
            pltpu.VMEM((1, chans), F32),
            pltpu.VMEM((1, chans), F32),
            pltpu.VMEM((frames, chans), BF16),
            pltpu.SemaphoreType.DMA((7,)),
        ],
        compiler_params=pltpu.CompilerParams(vmem_limit_bytes=32 << 20),
        name="step",
    )(
        lengths,
        waveform.reshape(frames, 10),
        rim,
        *(
            pltpu.with_memory_space_constraint(operand, pltpu.HBM)
            for operand in (
                conv0_weight,
                norm0_gain.reshape(1, chans),
                norm0_shift.reshape(1, chans),
                conv1_weight.reshape(3 * chans, chans),
                norm1_gain.reshape(1, chans),
                norm1_shift.reshape(1, chans),
                cotangent[0],
            )
        ),
    )
    mine = keep + lax.ppermute(send, "core", [(0, 1), (1, 0)])
    small_call = functools.partial(pl.pallas_call, compiler_params=pltpu.CompilerParams(vmem_limit_bytes=8 << 20))

    def stage(kernel, value, shapes, sums, operands=()):
        return small_call(
            kernel,
            out_shape=[shape(s, F32) for s in shapes],
            in_specs=[VMEM] * (1 + len(operands)),
            out_specs=[VMEM] * len(shapes),
            scratch_shapes=[pltpu.VMEM(sums, F32)],
            name=kernel.__name__,
        )(value, *operands)

    mine = lax.all_to_all(mine, AXES, 0, 0, axis_index_groups=cubes(0), tiled=True)
    (mine,) = stage(near_kernel, mine, [(8, 26, half)], (200, half))
    mine = lax.all_to_all(mine, AXES, 0, 0, axis_index_groups=cubes(1), tiled=True)
    (mine,) = stage(far_kernel, mine, [(8, 5, half)], (26, half))
    mine = lax.all_to_all(mine, FAR, 0, 0, tiled=True)
    message, kept = stage(share_kernel, mine, [(16, 3, half), (2, half)], (5, half))
    gathered = lax.all_to_all(message, ("core",) + CUBE, 0, 0, tiled=True)
    peer = (1 - lax.axis_index("core")) * 8 + lax.axis_index(CUBE)
    conv1_grad, small_grads = small_call(
        final_kernel,
        out_shape=[shape((3, half), F32), shape((14, chans), F32)],
        in_specs=[SMEM, VMEM, VMEM],
        out_specs=[VMEM, VMEM],
        name="final_kernel",
    )(peer.astype(jnp.int32).reshape(1), gathered, kept)
    return (features[None], conv1_grad.reshape(-1), small_grads)


def solution(mesh):
    torus = Mesh(mesh.devices.reshape(SHAPE), AXES)
    in_specs = (P(DP, AUDIO), P(DP), P(), P(), P(), P(), P(), P(), P(DP, AUDIO, None))
    out_specs = (P(DP, AUDIO, None), P(DP + AUDIO), P())
    return jax.shard_map(shards, mesh=torus, in_specs=in_specs, out_specs=out_specs, check_vma=False)
```

```python
import functools

import jax
import jax.numpy as jnp
import numpy as np
from jax import lax
from jax.experimental import pallas as pl
from jax.experimental.pallas import tpu as pltpu
from jax.sharding import Mesh
from jax.sharding import PartitionSpec as P

SHAPE = (2,) * 10
AXES = ("z2", "y2", "y1", "y0", "z1", "z0", "x2", "x1", "x0", "core")
DP, AUDIO = AXES[:4], AXES[4:]
CUBE = ("y0", "z0", "x0")
FAR = ("z2", "y2", "y1", "z1", "x2", "x1")
GROUP = 384
EPS = 1e-05
BF16, F32 = jnp.bfloat16, jnp.float32


def cubes():
    groups = {}
    for i in range(2 ** len(AXES)):
        at = dict(zip(AXES, (int(v) for v in np.unravel_index(i, SHAPE))))
        group, member = [at["core"]], 0
        for axis in "yzx":
            place = sum(at[f"{axis}{n}"] << n for n in range(3))
            group.append((place - at["core"]) % 8 // 2)
            member = member * 2 + place % 2
        groups.setdefault(tuple(group), [0] * 8)[member] = i
    return list(groups.values())


def row_order(place):
    chunk = (place * 171) >> 9
    row = place - 3 * chunk
    for source, target in ((6, 5), (5, 3), (4, 0), (3, 6), (2, 4), (1, 2), (0, 1)):
        row = row + (((chunk >> source) & 1) << target) * 3
    return row


def normal_cdf(v):
    return 0.5 + 0.5 * lax.erf(v * np.float32(0.5**0.5))


def normal_pdf(v):
    return jnp.exp(v * v * np.float32(-0.5)) * np.float32((2 * np.pi) ** -0.5)


def fill_patches(block_ref, rim_ref, ext_ref, xs_ref, start, length):
    frames = block_ref.shape[0]
    row = lax.broadcasted_iota(jnp.int32, (frames, 10), 0)
    lane = lax.broadcasted_iota(jnp.int32, (frames, 10), 1)
    ext_ref[...] = jnp.zeros_like(ext_ref)
    ext_ref[0:frames, 0:10] = jnp.where(start + row * 10 + lane < length, block_ref[...], 0.0)
    lane = lax.broadcasted_iota(jnp.int32, (1, 128), 1)
    rim = jnp.where((lane < 10) & (start + frames * 10 + lane < length), rim_ref[:, :128], 0.0)
    ext_ref[frames : frames + 1] = rim
    here, after = ext_ref[...], ext_ref[1 : frames + 1]
    lane = lax.broadcasted_iota(jnp.int32, (frames, 128), 1)
    later = jnp.where(lane < 5, after, 0.0)
    odd = pltpu.roll(jnp.where(lane >= 5, here[:frames], 0.0), 123, 1) + pltpu.roll(later, 5, 1)
    for at, value in ((0, odd), (frames, here)):
        value = value + pltpu.roll(value, 10, 1) + pltpu.roll(value, 20, 1)
        high = value.astype(BF16).astype(F32)
        lane = lax.broadcasted_iota(jnp.int32, value.shape, 1)
        xs_ref[at : at + value.shape[0]] = jnp.where(lane < 20, high, value - high).astype(BF16)


def step_kernel(
    frames,
    chunk,
    length_ref,
    block_ref,
    rim_ref,
    w0_hbm,
    gain0_hbm,
    shift0_hbm,
    w1_hbm,
    gain1_hbm,
    shift1_hbm,
    cot_hbm,
    feat_ref,
    keep_ref,
    send_ref,
    pre0_ref,
    xhat_ref,
    slope_ref,
    rstd_ref,
    even_ref,
    patch_ref,
    pre1_ref,
    d_ref,
    dact_ref,
    dhigh_ref,
    dlow_ref,
    small_ref,
    sides_ref,
    ext_ref,
    xs_ref,
    taps_ref,
    w0_ref,
    gain0_ref,
    shift0_ref,
    w1_ref,
    gain1_ref,
    shift1_ref,
    cot_ref,
    sems,
):
    arriving = []
    sources = (w0_hbm, gain0_hbm, shift0_hbm, w1_hbm, gain1_hbm, shift1_hbm, cot_hbm)
    targets = (w0_ref, gain0_ref, shift0_ref, w1_ref, gain1_ref, shift1_ref, cot_ref)
    for i, (source, target) in enumerate(zip(sources, targets)):
        arriving.append(pltpu.make_async_copy(source, target, sems.at[i]))
        arriving[-1].start()
    chans = w1_ref.shape[1]
    half = chans // 2
    rows = pre0_ref.shape[0]
    core = lax.axis_index("core")
    position = lax.axis_index(AUDIO)
    length = length_ref[0]
    fill_patches(block_ref, rim_ref, ext_ref, xs_ref, position * (frames * 10), length)
    xs = xs_ref[:, :30]
    arriving[0].wait()
    w0 = w0_ref[...]
    w0 = w0 - jnp.mean(w0, -1, keepdims=True)
    high = w0.astype(BF16).astype(F32)
    taps_ref[0:10] = high
    taps_ref[10:20] = w0 - high
    taps_ref[20:30] = high
    ws = taps_ref[0:30].astype(BF16)
    pre0_ref[...] = jnp.dot(xs, ws, preferred_element_type=F32)
    arriving[1].wait()
    arriving[2].wait()
    gain0 = jnp.broadcast_to(gain0_ref[...], (chunk, chans))
    shift0 = jnp.broadcast_to(shift0_ref[...], (chunk, chans))
    for at in range(0, rows, chunk):
        centred = pre0_ref[at : at + chunk]
        rstd = lax.rsqrt(jnp.mean(centred * centred, -1, keepdims=True) + EPS)
        xhat = centred * rstd
        v = xhat * gain0 + shift0
        cdf = normal_cdf(v)
        xhat_ref[at : at + chunk] = xhat
        slope_ref[at : at + chunk] = cdf + v * normal_pdf(v)
        rstd_ref[at : at + chunk] = jnp.broadcast_to(rstd, (chunk, 128))
        act = v * cdf
        if at < frames:
            patch_ref[at : at + chunk, chans : 2 * chans] = act.astype(BF16)
        else:
            even_ref[at - frames : at - frames + chunk] = act
    for at in range(0, frames, chunk):
        patch_ref[at : at + chunk, :chans] = even_ref[at : at + chunk].astype(BF16)
        patch_ref[at : at + chunk, 2 * chans :] = even_ref[at + 1 : at + 1 + chunk].astype(BF16)
    arriving[3].wait()
    pre1_ref[...] = jnp.dot(patch_ref[...], w1_ref[...], preferred_element_type=F32)
    for copy in arriving[4:]:
        copy.wait()
    gain1 = jnp.broadcast_to(gain1_ref[...], (chunk, chans))
    shift1 = jnp.broadcast_to(shift1_ref[...], (chunk, chans))
    sum_gain = jnp.zeros((chunk, chans), F32)
    sum_shift = jnp.zeros((chunk, chans), F32)
    for at in range(0, frames, chunk):
        pre = pre1_ref[at : at + chunk]
        centred = pre - jnp.mean(pre, -1, keepdims=True)
        rstd = lax.rsqrt(jnp.mean(centred * centred, -1, keepdims=True) + EPS)
        xhat = centred * rstd
        v = xhat * gain1 + shift1
        cdf = normal_cdf(v)
        frame = at + lax.broadcasted_iota(jnp.int32, (chunk, chans), 0)
        valid = (position * frames + frame) * 10 + 10 <= length
        feat_ref[at : at + chunk] = jnp.where(valid, v * cdf, 0.0).astype(BF16)
        dv = cot_ref[at : at + chunk].astype(F32) * (cdf + v * normal_pdf(v))
        dv = jnp.where(valid, dv, 0.0)
        sum_gain = sum_gain + dv * xhat
        sum_shift = sum_shift + dv
        dx = dv * gain1
        first = jnp.mean(dx, -1, keepdims=True)
        second = jnp.mean(dx * xhat, -1, keepdims=True)
        d = rstd * (dx - first - xhat * second)
        d_ref[at : at + chunk] = d.astype(BF16)
        left, right = d[:, :half], d[:, half:]
        sides_ref[at : at + chunk, :half] = jnp.where(core == 0, right, left).astype(BF16)
        sides_ref[at : at + chunk, half:] = jnp.where(core == 0, left, right).astype(BF16)
    small_ref[12:13] = jnp.sum(sum_gain, 0, keepdims=True)
    small_ref[13:14] = jnp.sum(sum_shift, 0, keepdims=True)
    small_ref[14:16] = jnp.zeros((2, chans), F32)

    source = lax.broadcasted_iota(jnp.int32, (GROUP, GROUP), 0)
    order = row_order(lax.broadcasted_iota(jnp.int32, (1, GROUP), 1))
    place = (source == order).astype(F32).astype(BF16)
    over_rows = (((0,), (0,)), ((), ()))
    part = GROUP // 8
    for group in range(3 * chans // GROUP):
        lanes = jnp.dot(patch_ref[:, group * GROUP : (group + 1) * GROUP], place, preferred_element_type=F32).astype(BF16)
        grad = lax.dot_general(lanes, sides_ref[...], over_rows, preferred_element_type=F32)
        for cube in range(8):
            block = grad[cube * part : (cube + 1) * part]
            send_ref[cube, group * part : (group + 1) * part] = block[:, :half]
            keep_ref[cube, group * part : (group + 1) * part] = block[:, half:]

    def spread(tap):
        return lax.dot_general(
            d_ref[...],
            w1_ref[tap * chans : (tap + 1) * chans],
            (((1,), (1,)), ((), ())),
            preferred_element_type=F32,
        )

    dact_ref[:frames] = spread(1)
    dact_ref[frames : 2 * frames] = spread(0)
    dact_ref[2 * frames :] = jnp.zeros((rows - 2 * frames, chans), F32)
    dact_ref[frames + 1 : 2 * frames + 1] += spread(2)
    sum_gain = jnp.zeros((chunk, chans), F32)
    sum_shift = jnp.zeros((chunk, chans), F32)
    for at in range(0, rows, chunk):
        xhat = xhat_ref[at : at + chunk]
        dv = dact_ref[at : at + chunk] * slope_ref[at : at + chunk]
        sum_gain = sum_gain + dv * xhat
        sum_shift = sum_shift + dv
        dx = dv * gain0
        first = jnp.mean(dx, -1, keepdims=True)
        second = jnp.mean(dx * xhat, -1, keepdims=True)
        d = rstd_ref[at : at + chunk, :1] * (dx - first - xhat * second)
        high = d.astype(BF16)
        dhigh_ref[at : at + chunk] = high
        dlow_ref[at : at + chunk] = (d - high.astype(F32)).astype(BF16)
    by_high = lax.dot_general(xs, dhigh_ref[...], over_rows, preferred_element_type=F32)
    by_low = lax.dot_general(xs, dlow_ref[...], over_rows, preferred_element_type=F32)
    small_ref[0:10] = by_high[0:10] + by_high[20:30] + by_low[0:10]
    small_ref[10:11] = jnp.sum(sum_gain, 0, keepdims=True)
    small_ref[11:12] = jnp.sum(sum_shift, 0, keepdims=True)
    last = keep_ref.shape[1] - 8
    for out_ref, owner in ((keep_ref, core), (send_ref, 1 - core)):
        for cube in range(8):
            row = small_ref[pl.ds(8 * owner + cube, 1)]
            out_ref[cube, last : last + 1] = row[:, :half]
            out_ref[cube, last + 1 : last + 2] = row[:, half:]
            out_ref[cube, last + 2 :] = jnp.zeros((6, half), F32)


def cube_kernel(cube_ref, out_ref, sum_ref):
    sum_ref[...] = jnp.sum(cube_ref[...], 0)
    half = sum_ref.shape[1]
    for target in range(64):
        for row in range(3):
            out_ref[target, :, row * half : (row + 1) * half] = sum_ref[3 * target + row : 3 * target + row + 1]
    for row in range(2):
        line = jnp.broadcast_to(sum_ref[192 + row : 193 + row][None], (64, 1, half))
        out_ref[:, :, (3 + row) * half : (4 + row) * half] = line


def share_kernel(far_ref, out_ref, kept_ref):
    total = jnp.sum(far_ref[...], 0)
    half = kept_ref.shape[1] // 2
    first = lax.axis_index("core") == 0
    a, b, c = (total[:, row * half : (row + 1) * half] for row in range(3))
    message = jnp.concatenate([total[:, 3 * half :], jnp.where(first, c, a)], 1)
    out_ref[...] = jnp.broadcast_to(message[None], out_ref.shape)
    kept_ref[:, :half] = jnp.where(first, a, b)
    kept_ref[:, half:] = jnp.where(first, b, c)


def final_kernel(peer_ref, all_ref, kept_ref, grad_ref, small_ref):
    half = kept_ref.shape[1] // 2
    got = all_ref[peer_ref[0]]
    grad_ref[:, :half] = kept_ref[:, :half]
    grad_ref[:, half : 2 * half] = got[:, 2 * half :]
    grad_ref[:, 2 * half :] = kept_ref[:, half:]
    for row in range(14):
        small_ref[row : row + 1] = all_ref[row, :, : 2 * half]


HBM = pl.BlockSpec(memory_space=pltpu.HBM)
VMEM = pl.BlockSpec(memory_space=pltpu.VMEM)
SMEM = pl.BlockSpec(memory_space=pltpu.SMEM)


def shards(
    waveform,
    lengths,
    conv0_weight,
    norm0_gain,
    norm0_shift,
    conv1_weight,
    norm1_gain,
    norm1_shift,
    cotangent,
):
    frames = waveform.shape[1] // 10
    chans = conv1_weight.shape[2]
    rows = 2 * frames + 16
    back = []
    for i in range(2 ** len(AXES)):
        if i % 2 ** len(AUDIO):
            back.append((i, i - 1))
    rim = lax.ppermute(waveform, AXES, back)
    half = chans // 2
    chunk = 16
    shape = jax.ShapeDtypeStruct
    features, keep, send = pl.pallas_call(
        functools.partial(step_kernel, frames, chunk),
        out_shape=(
            shape((frames, chans), BF16),
            shape((8, 200, half), F32),
            shape((8, 200, half), F32),
        ),
        in_specs=[SMEM] + [VMEM] * 2 + [HBM] * 7,
        out_specs=(VMEM,) * 3,
        scratch_shapes=[
            pltpu.VMEM((rows, chans), F32),
            pltpu.VMEM((rows, chans), F32),
            pltpu.VMEM((rows, chans), F32),
            pltpu.VMEM((rows, 128), F32),
            pltpu.VMEM((rows - frames, chans), F32),
            pltpu.VMEM((frames, 3 * chans), BF16),
            pltpu.VMEM((frames, chans), F32),
            pltpu.VMEM((frames, chans), BF16),
            pltpu.VMEM((rows, chans), F32),
            pltpu.VMEM((rows, chans), BF16),
            pltpu.VMEM((rows, chans), BF16),
            pltpu.VMEM((16, chans), F32),
            pltpu.VMEM((frames, chans), BF16),
            pltpu.VMEM((frames + 16, 128), F32),
            pltpu.VMEM((rows, 128), BF16),
            pltpu.VMEM((32, chans), F32),
            pltpu.VMEM((10, chans), F32),
            pltpu.VMEM((1, chans), F32),
            pltpu.VMEM((1, chans), F32),
            pltpu.VMEM((3 * chans, chans), BF16),
            pltpu.VMEM((1, chans), F32),
            pltpu.VMEM((1, chans), F32),
            pltpu.VMEM((frames, chans), BF16),
            pltpu.SemaphoreType.DMA((7,)),
        ],
        compiler_params=pltpu.CompilerParams(vmem_limit_bytes=32 << 20),
        name="step",
    )(
        lengths,
        waveform.reshape(frames, 10),
        rim,
        *(
            pltpu.with_memory_space_constraint(operand, pltpu.HBM)
            for operand in (
                conv0_weight,
                norm0_gain.reshape(1, chans),
                norm0_shift.reshape(1, chans),
                conv1_weight.reshape(3 * chans, chans),
                norm1_gain.reshape(1, chans),
                norm1_shift.reshape(1, chans),
                cotangent[0],
            )
        ),
    )
    mine = keep + lax.ppermute(send, "core", [(0, 1), (1, 0)])
    small_call = functools.partial(pl.pallas_call, compiler_params=pltpu.CompilerParams(vmem_limit_bytes=8 << 20))

    mine = lax.all_to_all(mine, AXES, 0, 0, axis_index_groups=cubes(), tiled=True)
    message = small_call(
        cube_kernel,
        out_shape=shape((64, 1, 5 * half), F32),
        in_specs=[VMEM],
        out_specs=VMEM,
        scratch_shapes=[pltpu.VMEM((200, half), F32)],
        name="cube_sum",
    )(mine)
    mine = lax.all_to_all(message, FAR, 0, 0, tiled=True)
    message, kept = small_call(
        share_kernel,
        out_shape=[shape((16, 1, 3 * half), F32), shape((1, 2 * half), F32)],
        in_specs=[VMEM],
        out_specs=[VMEM, VMEM],
        name="far_sum",
    )(mine)
    gathered = lax.all_to_all(message, ("core",) + CUBE, 0, 0, tiled=True)
    peer = (1 - lax.axis_index("core")) * 8 + lax.axis_index(CUBE)
    conv1_grad, small_grads = small_call(
        final_kernel,
        out_shape=[shape((1, 3 * half), F32), shape((14, chans), F32)],
        in_specs=[SMEM, VMEM, VMEM],
        out_specs=[VMEM, VMEM],
        name="outputs",
    )(peer.astype(jnp.int32).reshape(1), gathered, kept)
    return (features[None], conv1_grad.reshape(-1), small_grads)


def solution(mesh):
    torus = Mesh(mesh.devices.reshape(SHAPE), AXES)
    in_specs = (P(DP, AUDIO), P(DP), P(), P(), P(), P(), P(), P(), P(DP, AUDIO, None))
    out_specs = (P(DP, AUDIO, None), P(DP + AUDIO), P())
    return jax.shard_map(shards, mesh=torus, in_specs=in_specs, out_specs=out_specs, check_vma=False)
```

```python
import functools

import jax
import jax.numpy as jnp
import numpy as np
from jax import lax
from jax.experimental import pallas as pl
from jax.experimental.pallas import tpu as pltpu
from jax.sharding import Mesh
from jax.sharding import PartitionSpec as P

SHAPE = (2,) * 10
AXES = ("z2", "y2", "y1", "y0", "z1", "z0", "x2", "x1", "x0", "core")
DP, AUDIO = AXES[:4], AXES[4:]
CUBE = ("y0", "z0", "x0")
FAR = ("z2", "y2", "y1", "z1")
LAST = ("core", "y0", "z0", "x0", "x2", "x1")
GROUP = 384
EPS = 1e-05
BF16, F32 = jnp.bfloat16, jnp.float32


def cubes():
    groups = {}
    for i in range(2 ** len(AXES)):
        at = dict(zip(AXES, (int(v) for v in np.unravel_index(i, SHAPE))))
        group, member = [at["core"]], 0
        for axis in "yzx":
            place = sum(at[f"{axis}{n}"] << n for n in range(3))
            group.append((place - at["core"]) % 8 // 2)
            member = member * 2 + place % 2
        groups.setdefault(tuple(group), [0] * 8)[member] = i
    return list(groups.values())


def row_order(place):
    chunk = (place * 171) >> 9
    row = place - 3 * chunk
    for source, target in ((6, 5), (5, 3), (4, 0), (3, 6), (2, 4), (1, 2), (0, 1)):
        row = row + (((chunk >> source) & 1) << target) * 3
    return row


def normal_cdf(v):
    return 0.5 + 0.5 * lax.erf(v * np.float32(0.5**0.5))


def normal_pdf(v):
    return jnp.exp(v * v * np.float32(-0.5)) * np.float32((2 * np.pi) ** -0.5)


def fill_patches(block_ref, rim_ref, ext_ref, xs_ref, start, length):
    frames = block_ref.shape[0]
    row = lax.broadcasted_iota(jnp.int32, (frames, 10), 0)
    lane = lax.broadcasted_iota(jnp.int32, (frames, 10), 1)
    ext_ref[...] = jnp.zeros_like(ext_ref)
    ext_ref[0:frames, 0:10] = jnp.where(start + row * 10 + lane < length, block_ref[...], 0.0)
    lane = lax.broadcasted_iota(jnp.int32, (1, 128), 1)
    rim = jnp.where((lane < 10) & (start + frames * 10 + lane < length), rim_ref[:, :128], 0.0)
    ext_ref[frames : frames + 1] = rim
    here, after = ext_ref[...], ext_ref[1 : frames + 1]
    lane = lax.broadcasted_iota(jnp.int32, (frames, 128), 1)
    later = jnp.where(lane < 5, after, 0.0)
    odd = pltpu.roll(jnp.where(lane >= 5, here[:frames], 0.0), 123, 1) + pltpu.roll(later, 5, 1)
    for at, value in ((0, odd), (frames, here)):
        value = value + pltpu.roll(value, 10, 1) + pltpu.roll(value, 20, 1)
        high = value.astype(BF16).astype(F32)
        lane = lax.broadcasted_iota(jnp.int32, value.shape, 1)
        xs_ref[at : at + value.shape[0]] = jnp.where(lane < 20, high, value - high).astype(BF16)


def step_kernel(
    frames,
    chunk,
    length_ref,
    block_ref,
    rim_ref,
    w0_hbm,
    gain0_hbm,
    shift0_hbm,
    w1_hbm,
    gain1_hbm,
    shift1_hbm,
    cot_hbm,
    feat_ref,
    keep_ref,
    send_ref,
    pre0_ref,
    xhat_ref,
    slope_ref,
    rstd_ref,
    even_ref,
    patch_ref,
    pre1_ref,
    d_ref,
    dact_ref,
    dhigh_ref,
    dlow_ref,
    small_ref,
    sides_ref,
    ext_ref,
    xs_ref,
    taps_ref,
    w0_ref,
    gain0_ref,
    shift0_ref,
    w1_ref,
    gain1_ref,
    shift1_ref,
    cot_ref,
    sems,
):
    arriving = []
    sources = (w0_hbm, gain0_hbm, shift0_hbm, w1_hbm, gain1_hbm, shift1_hbm, cot_hbm)
    targets = (w0_ref, gain0_ref, shift0_ref, w1_ref, gain1_ref, shift1_ref, cot_ref)
    for i, (source, target) in enumerate(zip(sources, targets)):
        arriving.append(pltpu.make_async_copy(source, target, sems.at[i]))
        arriving[-1].start()
    chans = w1_ref.shape[1]
    half = chans // 2
    rows = pre0_ref.shape[0]
    core = lax.axis_index("core")
    position = lax.axis_index(AUDIO)
    length = length_ref[0]
    fill_patches(block_ref, rim_ref, ext_ref, xs_ref, position * (frames * 10), length)
    xs = xs_ref[:, :30]
    arriving[0].wait()
    w0 = w0_ref[...]
    w0 = w0 - jnp.mean(w0, -1, keepdims=True)
    high = w0.astype(BF16).astype(F32)
    taps_ref[0:10] = high
    taps_ref[10:20] = w0 - high
    taps_ref[20:30] = high
    ws = taps_ref[0:30].astype(BF16)
    pre0_ref[...] = jnp.dot(xs, ws, preferred_element_type=F32)
    arriving[1].wait()
    arriving[2].wait()
    gain0 = jnp.broadcast_to(gain0_ref[...], (chunk, chans))
    shift0 = jnp.broadcast_to(shift0_ref[...], (chunk, chans))
    for at in range(0, rows, chunk):
        centred = pre0_ref[at : at + chunk]
        rstd = lax.rsqrt(jnp.mean(centred * centred, -1, keepdims=True) + EPS)
        xhat = centred * rstd
        v = xhat * gain0 + shift0
        cdf = normal_cdf(v)
        xhat_ref[at : at + chunk] = xhat
        slope_ref[at : at + chunk] = cdf + v * normal_pdf(v)
        rstd_ref[at : at + chunk] = jnp.broadcast_to(rstd, (chunk, 128))
        act = v * cdf
        if at < frames:
            patch_ref[at : at + chunk, chans : 2 * chans] = act.astype(BF16)
        else:
            even_ref[at - frames : at - frames + chunk] = act
    for at in range(0, frames, chunk):
        patch_ref[at : at + chunk, :chans] = even_ref[at : at + chunk].astype(BF16)
        patch_ref[at : at + chunk, 2 * chans :] = even_ref[at + 1 : at + 1 + chunk].astype(BF16)
    arriving[3].wait()
    pre1_ref[...] = jnp.dot(patch_ref[...], w1_ref[...], preferred_element_type=F32)
    for copy in arriving[4:]:
        copy.wait()
    gain1 = jnp.broadcast_to(gain1_ref[...], (chunk, chans))
    shift1 = jnp.broadcast_to(shift1_ref[...], (chunk, chans))
    sum_gain = jnp.zeros((chunk, chans), F32)
    sum_shift = jnp.zeros((chunk, chans), F32)
    for at in range(0, frames, chunk):
        pre = pre1_ref[at : at + chunk]
        centred = pre - jnp.mean(pre, -1, keepdims=True)
        rstd = lax.rsqrt(jnp.mean(centred * centred, -1, keepdims=True) + EPS)
        xhat = centred * rstd
        v = xhat * gain1 + shift1
        cdf = normal_cdf(v)
        frame = at + lax.broadcasted_iota(jnp.int32, (chunk, chans), 0)
        valid = (position * frames + frame) * 10 + 10 <= length
        feat_ref[at : at + chunk] = jnp.where(valid, v * cdf, 0.0).astype(BF16)
        dv = cot_ref[at : at + chunk].astype(F32) * (cdf + v * normal_pdf(v))
        dv = jnp.where(valid, dv, 0.0)
        sum_gain = sum_gain + dv * xhat
        sum_shift = sum_shift + dv
        dx = dv * gain1
        first = jnp.mean(dx, -1, keepdims=True)
        second = jnp.mean(dx * xhat, -1, keepdims=True)
        d = rstd * (dx - first - xhat * second)
        d_ref[at : at + chunk] = d.astype(BF16)
        left, right = d[:, :half], d[:, half:]
        sides_ref[at : at + chunk, :half] = jnp.where(core == 0, right, left).astype(BF16)
        sides_ref[at : at + chunk, half:] = jnp.where(core == 0, left, right).astype(BF16)
    small_ref[12:13] = jnp.sum(sum_gain, 0, keepdims=True)
    small_ref[13:14] = jnp.sum(sum_shift, 0, keepdims=True)
    small_ref[14:16] = jnp.zeros((2, chans), F32)

    source = lax.broadcasted_iota(jnp.int32, (GROUP, GROUP), 0)
    order = row_order(lax.broadcasted_iota(jnp.int32, (1, GROUP), 1))
    place = (source == order).astype(F32).astype(BF16)
    over_rows = (((0,), (0,)), ((), ()))
    part = GROUP // 8
    for group in range(3 * chans // GROUP):
        lanes = jnp.dot(patch_ref[:, group * GROUP : (group + 1) * GROUP], place, preferred_element_type=F32).astype(BF16)
        grad = lax.dot_general(lanes, sides_ref[...], over_rows, preferred_element_type=F32)
        for cube in range(8):
            block = grad[cube * part : (cube + 1) * part]
            send_ref[cube, group * part : (group + 1) * part] = block[:, :half]
            keep_ref[cube, group * part : (group + 1) * part] = block[:, half:]

    def spread(tap):
        return lax.dot_general(
            d_ref[...],
            w1_ref[tap * chans : (tap + 1) * chans],
            (((1,), (1,)), ((), ())),
            preferred_element_type=F32,
        )

    dact_ref[:frames] = spread(1)
    dact_ref[frames : 2 * frames] = spread(0)
    dact_ref[2 * frames :] = jnp.zeros((rows - 2 * frames, chans), F32)
    dact_ref[frames + 1 : 2 * frames + 1] += spread(2)
    sum_gain = jnp.zeros((chunk, chans), F32)
    sum_shift = jnp.zeros((chunk, chans), F32)
    for at in range(0, rows, chunk):
        xhat = xhat_ref[at : at + chunk]
        dv = dact_ref[at : at + chunk] * slope_ref[at : at + chunk]
        sum_gain = sum_gain + dv * xhat
        sum_shift = sum_shift + dv
        dx = dv * gain0
        first = jnp.mean(dx, -1, keepdims=True)
        second = jnp.mean(dx * xhat, -1, keepdims=True)
        d = rstd_ref[at : at + chunk, :1] * (dx - first - xhat * second)
        high = d.astype(BF16)
        dhigh_ref[at : at + chunk] = high
        dlow_ref[at : at + chunk] = (d - high.astype(F32)).astype(BF16)
    by_high = lax.dot_general(xs, dhigh_ref[...], over_rows, preferred_element_type=F32)
    by_low = lax.dot_general(xs, dlow_ref[...], over_rows, preferred_element_type=F32)
    small_ref[0:10] = by_high[0:10] + by_high[20:30] + by_low[0:10]
    small_ref[10:11] = jnp.sum(sum_gain, 0, keepdims=True)
    small_ref[11:12] = jnp.sum(sum_shift, 0, keepdims=True)
    last = keep_ref.shape[1] - 8
    for out_ref, owner in ((keep_ref, core), (send_ref, 1 - core)):
        for cube in range(8):
            row = small_ref[pl.ds(8 * owner + cube, 1)]
            out_ref[cube, last : last + 1] = row[:, :half]
            out_ref[cube, last + 1 : last + 2] = row[:, half:]
            out_ref[cube, last + 2 :] = jnp.zeros((6, half), F32)


def cube_kernel(cube_ref, out_ref, sum_ref):
    sum_ref[...] = jnp.sum(cube_ref[...], 0)
    small = jnp.concatenate([sum_ref[192:194], jnp.zeros((2, sum_ref.shape[1]), F32)], 0)
    for target in range(16):
        out_ref[target, 0:12] = sum_ref[12 * target : 12 * target + 12]
        out_ref[target, 12:16] = small


def far_kernel(far_ref, out_ref, sum_ref):
    sum_ref[...] = jnp.sum(far_ref[...], 0)
    small = sum_ref[12:14]
    for core in range(2):
        for place in range(4):
            at = 3 * place + core
            message = jnp.concatenate([small, sum_ref[at : at + 2]], 0)
            for cube in range(8):
                out_ref[core * 32 + cube * 4 + place] = message


def last_kernel(all_ref, grad_ref, small_ref, sum_ref):
    half = all_ref.shape[2]
    sum_ref[...] = jnp.sum(all_ref[...].reshape(16, 4, 4, half), 1)
    core, cube = lax.axis_index("core"), lax.axis_index(CUBE)
    own = sum_ref[core * 8 + cube]
    other = sum_ref[(1 - core) * 8 + cube]
    grad_ref[0:half] = own[2]
    grad_ref[half : 2 * half] = jnp.where(core == 0, other[2], other[3])
    grad_ref[2 * half :] = own[3]
    for row in range(14):
        small_ref[row : row + 1, :half] = sum_ref[row, 0:1]
        small_ref[row : row + 1, half:] = sum_ref[row, 1:2]


HBM = pl.BlockSpec(memory_space=pltpu.HBM)
VMEM = pl.BlockSpec(memory_space=pltpu.VMEM)
SMEM = pl.BlockSpec(memory_space=pltpu.SMEM)


def shards(
    waveform,
    lengths,
    conv0_weight,
    norm0_gain,
    norm0_shift,
    conv1_weight,
    norm1_gain,
    norm1_shift,
    cotangent,
):
    frames = waveform.shape[1] // 10
    chans = conv1_weight.shape[2]
    rows = 2 * frames + 16
    back = []
    for i in range(2 ** len(AXES)):
        if i % 2 ** len(AUDIO):
            back.append((i, i - 1))
    rim = lax.ppermute(waveform, AXES, back)
    half = chans // 2
    chunk = 16
    shape = jax.ShapeDtypeStruct
    features, keep, send = pl.pallas_call(
        functools.partial(step_kernel, frames, chunk),
        out_shape=(
            shape((frames, chans), BF16),
            shape((8, 200, half), F32),
            shape((8, 200, half), F32),
        ),
        in_specs=[SMEM] + [VMEM] * 2 + [HBM] * 7,
        out_specs=(VMEM,) * 3,
        scratch_shapes=[
            pltpu.VMEM((rows, chans), F32),
            pltpu.VMEM((rows, chans), F32),
            pltpu.VMEM((rows, chans), F32),
            pltpu.VMEM((rows, 128), F32),
            pltpu.VMEM((rows - frames, chans), F32),
            pltpu.VMEM((frames, 3 * chans), BF16),
            pltpu.VMEM((frames, chans), F32),
            pltpu.VMEM((frames, chans), BF16),
            pltpu.VMEM((rows, chans), F32),
            pltpu.VMEM((rows, chans), BF16),
            pltpu.VMEM((rows, chans), BF16),
            pltpu.VMEM((16, chans), F32),
            pltpu.VMEM((frames, chans), BF16),
            pltpu.VMEM((frames + 16, 128), F32),
            pltpu.VMEM((rows, 128), BF16),
            pltpu.VMEM((32, chans), F32),
            pltpu.VMEM((10, chans), F32),
            pltpu.VMEM((1, chans), F32),
            pltpu.VMEM((1, chans), F32),
            pltpu.VMEM((3 * chans, chans), BF16),
            pltpu.VMEM((1, chans), F32),
            pltpu.VMEM((1, chans), F32),
            pltpu.VMEM((frames, chans), BF16),
            pltpu.SemaphoreType.DMA((7,)),
        ],
        compiler_params=pltpu.CompilerParams(vmem_limit_bytes=32 << 20),
        name="step",
    )(
        lengths,
        waveform.reshape(frames, 10),
        rim,
        *(
            pltpu.with_memory_space_constraint(operand, pltpu.HBM)
            for operand in (
                conv0_weight,
                norm0_gain.reshape(1, chans),
                norm0_shift.reshape(1, chans),
                conv1_weight.reshape(3 * chans, chans),
                norm1_gain.reshape(1, chans),
                norm1_shift.reshape(1, chans),
                cotangent[0],
            )
        ),
    )
    mine = keep + lax.ppermute(send, "core", [(0, 1), (1, 0)])
    small_call = functools.partial(pl.pallas_call, compiler_params=pltpu.CompilerParams(vmem_limit_bytes=8 << 20))

    def stage(kernel, value, shapes, sums):
        return small_call(
            kernel,
            out_shape=[shape(s, F32) for s in shapes],
            in_specs=[VMEM],
            out_specs=[VMEM] * len(shapes),
            scratch_shapes=[pltpu.VMEM(sums, F32)],
            name=kernel.__name__,
        )(value)

    mine = lax.all_to_all(mine, AXES, 0, 0, axis_index_groups=cubes(), tiled=True)
    (mine,) = stage(cube_kernel, mine, [(16, 16, half)], (200, half))
    mine = lax.all_to_all(mine, FAR, 0, 0, tiled=True)
    (mine,) = stage(far_kernel, mine, [(64, 4, half)], (16, half))
    mine = lax.all_to_all(mine, LAST, 0, 0, tiled=True)
    conv1_grad, small_grads = stage(last_kernel, mine, [(3 * half,), (14, chans)], (16, 4, half))
    return (features[None], conv1_grad, small_grads)


def solution(mesh):
    torus = Mesh(mesh.devices.reshape(SHAPE), AXES)
    in_specs = (P(DP, AUDIO), P(DP), P(), P(), P(), P(), P(), P(), P(DP, AUDIO, None))
    out_specs = (P(DP, AUDIO, None), P(DP + AUDIO), P())
    return jax.shard_map(shards, mesh=torus, in_specs=in_specs, out_specs=out_specs, check_vma=False)
```

```python
import functools

import jax
import jax.numpy as jnp
import numpy as np
from jax import lax
from jax.experimental import pallas as pl
from jax.experimental.pallas import tpu as pltpu
from jax.sharding import Mesh
from jax.sharding import PartitionSpec as P

SHAPE = (2,) * 10
AXES = ("z2", "y2", "y1", "y0", "z1", "z0", "x2", "x1", "x0", "core")
DP, AUDIO = AXES[:4], AXES[4:]
CUBE = ("y0", "z0", "x0")
FAR = ("z2", "y2", "y1", "z1", "x1")
LAST = ("core", "y0", "z0", "x0", "x2")
GROUP = 384
EPS = 1e-05
BF16, F32 = jnp.bfloat16, jnp.float32


def cubes():
    groups = {}
    for i in range(2 ** len(AXES)):
        at = dict(zip(AXES, (int(v) for v in np.unravel_index(i, SHAPE))))
        group, member = [at["core"]], 0
        for axis in "yzx":
            place = sum(at[f"{axis}{n}"] << n for n in range(3))
            group.append((place - at["core"]) % 8 // 2)
            member = member * 2 + place % 2
        groups.setdefault(tuple(group), [0] * 8)[member] = i
    return list(groups.values())


def row_order(place):
    chunk = (place * 171) >> 9
    row = place - 3 * chunk
    for source, target in ((6, 5), (5, 3), (4, 0), (3, 6), (2, 4), (1, 1), (0, 2)):
        row = row + (((chunk >> source) & 1) << target) * 3
    return row


def normal_cdf(v):
    return 0.5 + 0.5 * lax.erf(v * np.float32(0.5**0.5))


def normal_pdf(v):
    return jnp.exp(v * v * np.float32(-0.5)) * np.float32((2 * np.pi) ** -0.5)


def fill_patches(block_ref, rim_ref, ext_ref, xs_ref, start, length):
    frames = block_ref.shape[0]
    row = lax.broadcasted_iota(jnp.int32, (frames, 10), 0)
    lane = lax.broadcasted_iota(jnp.int32, (frames, 10), 1)
    ext_ref[...] = jnp.zeros_like(ext_ref)
    ext_ref[0:frames, 0:10] = jnp.where(start + row * 10 + lane < length, block_ref[...], 0.0)
    lane = lax.broadcasted_iota(jnp.int32, (1, 128), 1)
    rim = jnp.where((lane < 10) & (start + frames * 10 + lane < length), rim_ref[:, :128], 0.0)
    ext_ref[frames : frames + 1] = rim
    here, after = ext_ref[...], ext_ref[1 : frames + 1]
    lane = lax.broadcasted_iota(jnp.int32, (frames, 128), 1)
    later = jnp.where(lane < 5, after, 0.0)
    odd = pltpu.roll(jnp.where(lane >= 5, here[:frames], 0.0), 123, 1) + pltpu.roll(later, 5, 1)
    for at, value in ((0, odd), (frames, here)):
        value = value + pltpu.roll(value, 10, 1) + pltpu.roll(value, 20, 1)
        high = value.astype(BF16).astype(F32)
        lane = lax.broadcasted_iota(jnp.int32, value.shape, 1)
        xs_ref[at : at + value.shape[0]] = jnp.where(lane < 20, high, value - high).astype(BF16)


def step_kernel(
    frames,
    chunk,
    length_ref,
    block_ref,
    rim_ref,
    w0_hbm,
    gain0_hbm,
    shift0_hbm,
    w1_hbm,
    gain1_hbm,
    shift1_hbm,
    cot_hbm,
    feat_hbm,
    keep_ref,
    send_ref,
    pre0_ref,
    xhat_ref,
    slope_ref,
    rstd_ref,
    even_ref,
    patch_ref,
    pre1_ref,
    d_ref,
    dact_ref,
    dhigh_ref,
    dlow_ref,
    small_ref,
    sides_ref,
    ext_ref,
    xs_ref,
    taps_ref,
    w0_ref,
    gain0_ref,
    shift0_ref,
    w1_ref,
    gain1_ref,
    shift1_ref,
    cot_ref,
    feat_ref,
    sems,
):
    arriving = []
    sources = (w0_hbm, gain0_hbm, shift0_hbm, w1_hbm, gain1_hbm, shift1_hbm, cot_hbm)
    targets = (w0_ref, gain0_ref, shift0_ref, w1_ref, gain1_ref, shift1_ref, cot_ref)
    for i, (source, target) in enumerate(zip(sources, targets)):
        arriving.append(pltpu.make_async_copy(source, target, sems.at[i]))
        arriving[-1].start()
    chans = w1_ref.shape[1]
    half = chans // 2
    rows = pre0_ref.shape[0]
    core = lax.axis_index("core")
    position = lax.axis_index(AUDIO)
    length = length_ref[0]
    fill_patches(block_ref, rim_ref, ext_ref, xs_ref, position * (frames * 10), length)
    xs = xs_ref[:, :30]
    arriving[0].wait()
    w0 = w0_ref[...]
    w0 = w0 - jnp.mean(w0, -1, keepdims=True)
    high = w0.astype(BF16).astype(F32)
    taps_ref[0:10] = high
    taps_ref[10:20] = w0 - high
    taps_ref[20:30] = high
    ws = taps_ref[0:30].astype(BF16)
    pre0_ref[...] = jnp.dot(xs, ws, preferred_element_type=F32)
    arriving[1].wait()
    arriving[2].wait()
    gain0 = jnp.broadcast_to(gain0_ref[...], (chunk, chans))
    shift0 = jnp.broadcast_to(shift0_ref[...], (chunk, chans))
    for at in range(0, rows, chunk):
        centred = pre0_ref[at : at + chunk]
        rstd = lax.rsqrt(jnp.mean(centred * centred, -1, keepdims=True) + EPS)
        xhat = centred * rstd
        v = xhat * gain0 + shift0
        cdf = normal_cdf(v)
        xhat_ref[at : at + chunk] = xhat
        slope_ref[at : at + chunk] = cdf + v * normal_pdf(v)
        rstd_ref[at : at + chunk] = jnp.broadcast_to(rstd, (chunk, 128))
        act = v * cdf
        if at < frames:
            patch_ref[at : at + chunk, chans : 2 * chans] = act.astype(BF16)
        else:
            even_ref[at - frames : at - frames + chunk] = act
    for at in range(0, frames, chunk):
        patch_ref[at : at + chunk, :chans] = even_ref[at : at + chunk].astype(BF16)
        patch_ref[at : at + chunk, 2 * chans :] = even_ref[at + 1 : at + 1 + chunk].astype(BF16)
    arriving[3].wait()
    pre1_ref[...] = jnp.dot(patch_ref[...], w1_ref[...], preferred_element_type=F32)
    for copy in arriving[4:]:
        copy.wait()
    gain1 = jnp.broadcast_to(gain1_ref[...], (chunk, chans))
    shift1 = jnp.broadcast_to(shift1_ref[...], (chunk, chans))
    sum_gain = jnp.zeros((chunk, chans), F32)
    sum_shift = jnp.zeros((chunk, chans), F32)
    for at in range(0, frames, chunk):
        pre = pre1_ref[at : at + chunk]
        centred = pre - jnp.mean(pre, -1, keepdims=True)
        rstd = lax.rsqrt(jnp.mean(centred * centred, -1, keepdims=True) + EPS)
        xhat = centred * rstd
        v = xhat * gain1 + shift1
        cdf = normal_cdf(v)
        frame = at + lax.broadcasted_iota(jnp.int32, (chunk, chans), 0)
        valid = (position * frames + frame) * 10 + 10 <= length
        feat_ref[at : at + chunk] = jnp.where(valid, v * cdf, 0.0).astype(BF16)
        dv = cot_ref[at : at + chunk].astype(F32) * (cdf + v * normal_pdf(v))
        dv = jnp.where(valid, dv, 0.0)
        sum_gain = sum_gain + dv * xhat
        sum_shift = sum_shift + dv
        dx = dv * gain1
        first = jnp.mean(dx, -1, keepdims=True)
        second = jnp.mean(dx * xhat, -1, keepdims=True)
        d = rstd * (dx - first - xhat * second)
        d_ref[at : at + chunk] = d.astype(BF16)
        left, right = d[:, :half], d[:, half:]
        sides_ref[at : at + chunk, :half] = jnp.where(core == 0, right, left).astype(BF16)
        sides_ref[at : at + chunk, half:] = jnp.where(core == 0, left, right).astype(BF16)
    leaving = pltpu.make_async_copy(feat_ref, feat_hbm, sems.at[7])
    leaving.start()
    small_ref[12:13] = jnp.sum(sum_gain, 0, keepdims=True)
    small_ref[13:14] = jnp.sum(sum_shift, 0, keepdims=True)
    small_ref[14:16] = jnp.zeros((2, chans), F32)

    source = lax.broadcasted_iota(jnp.int32, (GROUP, GROUP), 0)
    order = row_order(lax.broadcasted_iota(jnp.int32, (1, GROUP), 1))
    place = (source == order).astype(F32).astype(BF16)
    over_rows = (((0,), (0,)), ((), ()))
    part = GROUP // 8
    for group in range(3 * chans // GROUP):
        lanes = jnp.dot(patch_ref[:, group * GROUP : (group + 1) * GROUP], place, preferred_element_type=F32).astype(BF16)
        grad = lax.dot_general(lanes, sides_ref[...], over_rows, preferred_element_type=F32)
        for cube in range(8):
            block = grad[cube * part : (cube + 1) * part]
            send_ref[cube, group * part : (group + 1) * part] = block[:, :half]
            keep_ref[cube, group * part : (group + 1) * part] = block[:, half:]

    def spread(tap):
        return lax.dot_general(
            d_ref[...],
            w1_ref[tap * chans : (tap + 1) * chans],
            (((1,), (1,)), ((), ())),
            preferred_element_type=F32,
        )

    dact_ref[:frames] = spread(1)
    dact_ref[frames : 2 * frames] = spread(0)
    dact_ref[2 * frames :] = jnp.zeros((rows - 2 * frames, chans), F32)
    dact_ref[frames + 1 : 2 * frames + 1] += spread(2)
    sum_gain = jnp.zeros((chunk, chans), F32)
    sum_shift = jnp.zeros((chunk, chans), F32)
    for at in range(0, rows, chunk):
        xhat = xhat_ref[at : at + chunk]
        dv = dact_ref[at : at + chunk] * slope_ref[at : at + chunk]
        sum_gain = sum_gain + dv * xhat
        sum_shift = sum_shift + dv
        dx = dv * gain0
        first = jnp.mean(dx, -1, keepdims=True)
        second = jnp.mean(dx * xhat, -1, keepdims=True)
        d = rstd_ref[at : at + chunk, :1] * (dx - first - xhat * second)
        high = d.astype(BF16)
        dhigh_ref[at : at + chunk] = high
        dlow_ref[at : at + chunk] = (d - high.astype(F32)).astype(BF16)
    by_high = lax.dot_general(xs, dhigh_ref[...], over_rows, preferred_element_type=F32)
    by_low = lax.dot_general(xs, dlow_ref[...], over_rows, preferred_element_type=F32)
    small_ref[0:10] = by_high[0:10] + by_high[20:30] + by_low[0:10]
    small_ref[10:11] = jnp.sum(sum_gain, 0, keepdims=True)
    small_ref[11:12] = jnp.sum(sum_shift, 0, keepdims=True)
    last = keep_ref.shape[1] - 8
    for out_ref, owner in ((keep_ref, core), (send_ref, 1 - core)):
        for cube in range(8):
            row = small_ref[pl.ds(8 * owner + cube, 1)]
            out_ref[cube, last : last + 1] = row[:, :half]
            out_ref[cube, last + 1 : last + 2] = row[:, half:]
            out_ref[cube, last + 2 :] = jnp.zeros((6, half), F32)
    leaving.wait()


def cube_kernel(cube_ref, out_ref, sum_ref):
    sum_ref[...] = jnp.sum(cube_ref[...], 0)
    for target in range(32):
        out_ref[target, 0:6] = sum_ref[6 * target : 6 * target + 6]
        out_ref[target, 6:8] = sum_ref[192:194]


def far_kernel(far_ref, out_ref, sum_ref):
    sum_ref[...] = jnp.sum(far_ref[...], 0)
    small = sum_ref[6:8]
    for core in range(2):
        for place in range(2):
            at = 3 * place + core
            message = jnp.concatenate([small, sum_ref[at : at + 2]], 0)
            for cube in range(8):
                out_ref[core * 16 + cube * 2 + place] = message


def last_kernel(all_ref, grad_ref, small_ref, sum_ref):
    half = all_ref.shape[2]
    sum_ref[...] = jnp.sum(all_ref[...].reshape(16, 2, 4, half), 1)
    core, cube = lax.axis_index("core"), lax.axis_index(CUBE)
    own = sum_ref[core * 8 + cube]
    other = sum_ref[(1 - core) * 8 + cube]
    grad_ref[0:half] = own[2]
    grad_ref[half : 2 * half] = jnp.where(core == 0, other[2], other[3])
    grad_ref[2 * half :] = own[3]
    for row in range(14):
        small_ref[row : row + 1, :half] = sum_ref[row, 0:1]
        small_ref[row : row + 1, half:] = sum_ref[row, 1:2]


HBM = pl.BlockSpec(memory_space=pltpu.HBM)
VMEM = pl.BlockSpec(memory_space=pltpu.VMEM)
SMEM = pl.BlockSpec(memory_space=pltpu.SMEM)


def shards(
    waveform,
    lengths,
    conv0_weight,
    norm0_gain,
    norm0_shift,
    conv1_weight,
    norm1_gain,
    norm1_shift,
    cotangent,
):
    frames = waveform.shape[1] // 10
    chans = conv1_weight.shape[2]
    rows = 2 * frames + 16
    back = []
    for i in range(2 ** len(AXES)):
        if i % 2 ** len(AUDIO):
            back.append((i, i - 1))
    rim = lax.ppermute(waveform, AXES, back)
    half = chans // 2
    chunk = 16
    shape = jax.ShapeDtypeStruct
    features, keep, send = pl.pallas_call(
        functools.partial(step_kernel, frames, chunk),
        out_shape=(
            shape((frames, chans), BF16),
            shape((8, 200, half), F32),
            shape((8, 200, half), F32),
        ),
        in_specs=[SMEM] + [VMEM] * 2 + [HBM] * 7,
        out_specs=(HBM, VMEM, VMEM),
        scratch_shapes=[
            pltpu.VMEM((rows, chans), F32),
            pltpu.VMEM((rows, chans), F32),
            pltpu.VMEM((rows, chans), F32),
            pltpu.VMEM((rows, 128), F32),
            pltpu.VMEM((rows - frames, chans), F32),
            pltpu.VMEM((frames, 3 * chans), BF16),
            pltpu.VMEM((frames, chans), F32),
            pltpu.VMEM((frames, chans), BF16),
            pltpu.VMEM((rows, chans), F32),
            pltpu.VMEM((rows, chans), BF16),
            pltpu.VMEM((rows, chans), BF16),
            pltpu.VMEM((16, chans), F32),
            pltpu.VMEM((frames, chans), BF16),
            pltpu.VMEM((frames + 16, 128), F32),
            pltpu.VMEM((rows, 128), BF16),
            pltpu.VMEM((32, chans), F32),
            pltpu.VMEM((10, chans), F32),
            pltpu.VMEM((1, chans), F32),
            pltpu.VMEM((1, chans), F32),
            pltpu.VMEM((3 * chans, chans), BF16),
            pltpu.VMEM((1, chans), F32),
            pltpu.VMEM((1, chans), F32),
            pltpu.VMEM((frames, chans), BF16),
            pltpu.VMEM((frames, chans), BF16),
            pltpu.SemaphoreType.DMA((8,)),
        ],
        compiler_params=pltpu.CompilerParams(vmem_limit_bytes=32 << 20),
        name="step",
    )(
        lengths,
        waveform.reshape(frames, 10),
        rim,
        *(
            pltpu.with_memory_space_constraint(operand, pltpu.HBM)
            for operand in (
                conv0_weight,
                norm0_gain.reshape(1, chans),
                norm0_shift.reshape(1, chans),
                conv1_weight.reshape(3 * chans, chans),
                norm1_gain.reshape(1, chans),
                norm1_shift.reshape(1, chans),
                cotangent[0],
            )
        ),
    )
    mine = keep + lax.ppermute(send, "core", [(0, 1), (1, 0)])
    small_call = functools.partial(pl.pallas_call, compiler_params=pltpu.CompilerParams(vmem_limit_bytes=8 << 20))

    def stage(kernel, value, shapes, sums):
        return small_call(
            kernel,
            out_shape=[shape(s, F32) for s in shapes],
            in_specs=[VMEM],
            out_specs=[VMEM] * len(shapes),
            scratch_shapes=[pltpu.VMEM(sums, F32)],
            name=kernel.__name__,
        )(value)

    mine = lax.all_to_all(mine, AXES, 0, 0, axis_index_groups=cubes(), tiled=True)
    (mine,) = stage(cube_kernel, mine, [(32, 8, half)], (200, half))
    mine = lax.all_to_all(mine, FAR, 0, 0, tiled=True)
    (mine,) = stage(far_kernel, mine, [(32, 4, half)], (8, half))
    mine = lax.all_to_all(mine, LAST, 0, 0, tiled=True)
    conv1_grad, small_grads = stage(last_kernel, mine, [(3 * half,), (14, chans)], (16, 4, half))
    return (features[None], conv1_grad, small_grads)


def solution(mesh):
    torus = Mesh(mesh.devices.reshape(SHAPE), AXES)
    in_specs = (P(DP, AUDIO), P(DP), P(), P(), P(), P(), P(), P(), P(DP, AUDIO, None))
    out_specs = (P(DP, AUDIO, None), P(DP + AUDIO), P())
    return jax.shard_map(shards, mesh=torus, in_specs=in_specs, out_specs=out_specs, check_vma=False)
```

```python
import functools

import jax
import jax.numpy as jnp
import numpy as np
from jax import lax
from jax.experimental import pallas as pl
from jax.experimental.pallas import tpu as pltpu
from jax.sharding import Mesh
from jax.sharding import PartitionSpec as P

SHAPE = (2,) * 10
AXES = ("z2", "y2", "y1", "y0", "z1", "z0", "x2", "x1", "x0", "core")
DP, AUDIO = AXES[:4], AXES[4:]
CUBE = ("y0", "z0", "x0")
FAR = ("z2", "y2", "y1", "z1", "x1")
LAST = ("core", "y0", "z0", "x0", "x2")
GROUP = 384
EPS = 1e-05
BF16, F32 = jnp.bfloat16, jnp.float32


def cubes():
    groups = {}
    for i in range(2 ** len(AXES)):
        at = dict(zip(AXES, (int(v) for v in np.unravel_index(i, SHAPE))))
        group, member = [at["core"]], 0
        for axis in "yzx":
            place = sum(at[f"{axis}{n}"] << n for n in range(3))
            group.append((place - at["core"]) % 8 // 2)
            member = member * 2 + place % 2
        groups.setdefault(tuple(group), [0] * 8)[member] = i
    return list(groups.values())


def row_order(place):
    chunk = (place * 171) >> 9
    row = place - 3 * chunk
    for source, target in ((6, 5), (5, 3), (4, 0), (3, 6), (2, 4), (1, 1), (0, 2)):
        row = row + (((chunk >> source) & 1) << target) * 3
    return row


def normal_cdf(v):
    return 0.5 + 0.5 * lax.erf(v * np.float32(0.5**0.5))


def normal_pdf(v):
    return jnp.exp(v * v * np.float32(-0.5)) * np.float32((2 * np.pi) ** -0.5)


def fill_patches(block_ref, rim_ref, ext_ref, xs_ref, start, length):
    frames = block_ref.shape[0]
    row = lax.broadcasted_iota(jnp.int32, (frames, 10), 0)
    lane = lax.broadcasted_iota(jnp.int32, (frames, 10), 1)
    ext_ref[...] = jnp.zeros_like(ext_ref)
    ext_ref[0:frames, 0:10] = jnp.where(start + row * 10 + lane < length, block_ref[...], 0.0)
    lane = lax.broadcasted_iota(jnp.int32, (1, 128), 1)
    rim = jnp.where((lane < 10) & (start + frames * 10 + lane < length), rim_ref[:, :128], 0.0)
    ext_ref[frames : frames + 1] = rim
    here, after = ext_ref[...], ext_ref[1 : frames + 1]
    lane = lax.broadcasted_iota(jnp.int32, (frames, 128), 1)
    later = jnp.where(lane < 5, after, 0.0)
    odd = pltpu.roll(jnp.where(lane >= 5, here[:frames], 0.0), 123, 1) + pltpu.roll(later, 5, 1)
    for at, value in ((0, odd), (frames, here)):
        value = value + pltpu.roll(value, 10, 1) + pltpu.roll(value, 20, 1)
        high = value.astype(BF16).astype(F32)
        lane = lax.broadcasted_iota(jnp.int32, value.shape, 1)
        xs_ref[at : at + value.shape[0]] = jnp.where(lane < 20, high, value - high).astype(BF16)


def step_kernel(
    frames,
    chunk,
    length_ref,
    block_ref,
    rim_ref,
    w0_hbm,
    gain0_hbm,
    shift0_hbm,
    w1_hbm,
    gain1_hbm,
    shift1_hbm,
    cot_hbm,
    feat_hbm,
    keep_ref,
    send_ref,
    pre0_ref,
    xhat_ref,
    slope_ref,
    rstd_ref,
    even_ref,
    patch_ref,
    pre1_ref,
    d_ref,
    dact_ref,
    dhigh_ref,
    dlow_ref,
    small_ref,
    sides_ref,
    ext_ref,
    xs_ref,
    taps_ref,
    w0_ref,
    gain0_ref,
    shift0_ref,
    w1_ref,
    gain1_ref,
    shift1_ref,
    cot_ref,
    feat_ref,
    sems,
):
    arriving = []
    sources = (w0_hbm, gain0_hbm, shift0_hbm, w1_hbm, gain1_hbm, shift1_hbm, cot_hbm)
    targets = (w0_ref, gain0_ref, shift0_ref, w1_ref, gain1_ref, shift1_ref, cot_ref)
    for i, (source, target) in enumerate(zip(sources, targets)):
        arriving.append(pltpu.make_async_copy(source, target, sems.at[i]))
        arriving[-1].start()
    chans = w1_ref.shape[1]
    half = chans // 2
    rows = pre0_ref.shape[0]
    core = lax.axis_index("core")
    position = lax.axis_index(AUDIO)
    length = length_ref[0]
    fill_patches(block_ref, rim_ref, ext_ref, xs_ref, position * (frames * 10), length)
    xs = xs_ref[:, :30]
    arriving[0].wait()
    w0 = w0_ref[...]
    w0 = w0 - jnp.mean(w0, -1, keepdims=True)
    high = w0.astype(BF16).astype(F32)
    taps_ref[0:10] = high
    taps_ref[10:20] = w0 - high
    taps_ref[20:30] = high
    ws = taps_ref[0:30].astype(BF16)
    pre0_ref[...] = jnp.dot(xs, ws, preferred_element_type=F32)
    arriving[1].wait()
    arriving[2].wait()
    gain0 = jnp.broadcast_to(gain0_ref[...], (chunk, chans))
    shift0 = jnp.broadcast_to(shift0_ref[...], (chunk, chans))
    for at in range(0, rows, chunk):
        centred = pre0_ref[at : at + chunk]
        rstd = lax.rsqrt(jnp.mean(centred * centred, -1, keepdims=True) + EPS)
        xhat = centred * rstd
        v = xhat * gain0 + shift0
        cdf = normal_cdf(v)
        xhat_ref[at : at + chunk] = xhat
        slope_ref[at : at + chunk] = cdf + v * normal_pdf(v)
        rstd_ref[at : at + chunk] = jnp.broadcast_to(rstd, (chunk, 128))
        act = v * cdf
        if at < frames:
            patch_ref[at : at + chunk, chans : 2 * chans] = act.astype(BF16)
        else:
            even_ref[at - frames : at - frames + chunk] = act
    for at in range(0, frames, chunk):
        patch_ref[at : at + chunk, :chans] = even_ref[at : at + chunk].astype(BF16)
        patch_ref[at : at + chunk, 2 * chans :] = even_ref[at + 1 : at + 1 + chunk].astype(BF16)
    arriving[3].wait()
    pre1_ref[...] = jnp.dot(patch_ref[...], w1_ref[...], preferred_element_type=F32)
    for copy in arriving[4:]:
        copy.wait()
    source = lax.broadcasted_iota(jnp.int32, (GROUP, GROUP), 1)
    order = row_order(lax.broadcasted_iota(jnp.int32, (GROUP, 1), 0))
    place = (source == order).astype(F32).astype(BF16)
    columns = []
    for group in range(3 * chans // GROUP):
        lanes = patch_ref[:, group * GROUP : (group + 1) * GROUP]
        turned = lax.dot_general(place, lanes, (((1,), (1,)), ((), ())), preferred_element_type=F32)
        columns.append(turned.astype(BF16))
    gain1 = jnp.broadcast_to(gain1_ref[...], (chunk, chans))
    shift1 = jnp.broadcast_to(shift1_ref[...], (chunk, chans))
    sum_gain = jnp.zeros((chunk, chans), F32)
    sum_shift = jnp.zeros((chunk, chans), F32)
    for at in range(0, frames, chunk):
        pre = pre1_ref[at : at + chunk]
        centred = pre - jnp.mean(pre, -1, keepdims=True)
        rstd = lax.rsqrt(jnp.mean(centred * centred, -1, keepdims=True) + EPS)
        xhat = centred * rstd
        v = xhat * gain1 + shift1
        cdf = normal_cdf(v)
        frame = at + lax.broadcasted_iota(jnp.int32, (chunk, chans), 0)
        valid = (position * frames + frame) * 10 + 10 <= length
        feat_ref[at : at + chunk] = jnp.where(valid, v * cdf, 0.0).astype(BF16)
        dv = cot_ref[at : at + chunk].astype(F32) * (cdf + v * normal_pdf(v))
        dv = jnp.where(valid, dv, 0.0)
        sum_gain = sum_gain + dv * xhat
        sum_shift = sum_shift + dv
        dx = dv * gain1
        first = jnp.mean(dx, -1, keepdims=True)
        second = jnp.mean(dx * xhat, -1, keepdims=True)
        d = rstd * (dx - first - xhat * second)
        d_ref[at : at + chunk] = d.astype(BF16)
        left, right = d[:, :half], d[:, half:]
        sides_ref[at : at + chunk, :half] = jnp.where(core == 0, right, left).astype(BF16)
        sides_ref[at : at + chunk, half:] = jnp.where(core == 0, left, right).astype(BF16)
    leaving = pltpu.make_async_copy(feat_ref, feat_hbm, sems.at[7])
    leaving.start()
    small_ref[12:13] = jnp.sum(sum_gain, 0, keepdims=True)
    small_ref[13:14] = jnp.sum(sum_shift, 0, keepdims=True)
    small_ref[14:16] = jnp.zeros((2, chans), F32)

    part = GROUP // 8

    def second_gradient(group):
        grad = jnp.dot(columns[group], sides_ref[...], preferred_element_type=F32)
        for cube in range(8):
            block = grad[cube * part : (cube + 1) * part]
            send_ref[cube, group * part : (group + 1) * part] = block[:, :half]
            keep_ref[cube, group * part : (group + 1) * part] = block[:, half:]

    over_rows = (((0,), (0,)), ((), ()))

    def spread(tap):
        return lax.dot_general(
            d_ref[...],
            w1_ref[tap * chans : (tap + 1) * chans],
            (((1,), (1,)), ((), ())),
            preferred_element_type=F32,
        )

    dact_ref[:frames] = spread(1)
    dact_ref[frames : 2 * frames] = spread(0)
    dact_ref[2 * frames :] = jnp.zeros((rows - 2 * frames, chans), F32)
    dact_ref[frames + 1 : 2 * frames + 1] += spread(2)
    sum_gain = jnp.zeros((chunk, chans), F32)
    sum_shift = jnp.zeros((chunk, chans), F32)
    for at in range(0, rows, chunk):
        if at % (5 * chunk) == 0 and at // (5 * chunk) < len(columns):
            second_gradient(at // (5 * chunk))
        xhat = xhat_ref[at : at + chunk]
        dv = dact_ref[at : at + chunk] * slope_ref[at : at + chunk]
        sum_gain = sum_gain + dv * xhat
        sum_shift = sum_shift + dv
        dx = dv * gain0
        first = jnp.mean(dx, -1, keepdims=True)
        second = jnp.mean(dx * xhat, -1, keepdims=True)
        d = rstd_ref[at : at + chunk, :1] * (dx - first - xhat * second)
        high = d.astype(BF16)
        dhigh_ref[at : at + chunk] = high
        dlow_ref[at : at + chunk] = (d - high.astype(F32)).astype(BF16)
    by_high = lax.dot_general(xs, dhigh_ref[...], over_rows, preferred_element_type=F32)
    by_low = lax.dot_general(xs, dlow_ref[...], over_rows, preferred_element_type=F32)
    small_ref[0:10] = by_high[0:10] + by_high[20:30] + by_low[0:10]
    small_ref[10:11] = jnp.sum(sum_gain, 0, keepdims=True)
    small_ref[11:12] = jnp.sum(sum_shift, 0, keepdims=True)
    last = keep_ref.shape[1] - 8
    for out_ref, owner in ((keep_ref, core), (send_ref, 1 - core)):
        for cube in range(8):
            row = small_ref[pl.ds(8 * owner + cube, 1)]
            out_ref[cube, last : last + 1] = row[:, :half]
            out_ref[cube, last + 1 : last + 2] = row[:, half:]
            out_ref[cube, last + 2 :] = jnp.zeros((6, half), F32)
    leaving.wait()


def cube_kernel(cube_ref, out_ref, sum_ref):
    sum_ref[...] = jnp.sum(cube_ref[...], 0)
    for target in range(32):
        out_ref[target, 0:6] = sum_ref[6 * target : 6 * target + 6]
        out_ref[target, 6:8] = sum_ref[192:194]


def far_kernel(far_ref, out_ref, sum_ref):
    sum_ref[...] = jnp.sum(far_ref[...], 0)
    small = sum_ref[6:8]
    for core in range(2):
        for place in range(2):
            at = 3 * place + core
            message = jnp.concatenate([small, sum_ref[at : at + 2]], 0)
            for cube in range(8):
                out_ref[core * 16 + cube * 2 + place] = message


def last_kernel(all_ref, grad_ref, small_ref, sum_ref):
    half = all_ref.shape[2]
    sum_ref[...] = jnp.sum(all_ref[...].reshape(16, 2, 4, half), 1)
    core, cube = lax.axis_index("core"), lax.axis_index(CUBE)
    own = sum_ref[core * 8 + cube]
    other = sum_ref[(1 - core) * 8 + cube]
    grad_ref[0:half] = own[2]
    grad_ref[half : 2 * half] = jnp.where(core == 0, other[2], other[3])
    grad_ref[2 * half :] = own[3]
    for row in range(14):
        small_ref[row : row + 1, :half] = sum_ref[row, 0:1]
        small_ref[row : row + 1, half:] = sum_ref[row, 1:2]


HBM = pl.BlockSpec(memory_space=pltpu.HBM)
VMEM = pl.BlockSpec(memory_space=pltpu.VMEM)
SMEM = pl.BlockSpec(memory_space=pltpu.SMEM)


def shards(
    waveform,
    lengths,
    conv0_weight,
    norm0_gain,
    norm0_shift,
    conv1_weight,
    norm1_gain,
    norm1_shift,
    cotangent,
):
    frames = waveform.shape[1] // 10
    chans = conv1_weight.shape[2]
    rows = 2 * frames + 16
    back = []
    for i in range(2 ** len(AXES)):
        if i % 2 ** len(AUDIO):
            back.append((i, i - 1))
    rim = lax.ppermute(waveform, AXES, back)
    half = chans // 2
    chunk = 16
    shape = jax.ShapeDtypeStruct
    features, keep, send = pl.pallas_call(
        functools.partial(step_kernel, frames, chunk),
        out_shape=(
            shape((frames, chans), BF16),
            shape((8, 200, half), F32),
            shape((8, 200, half), F32),
        ),
        in_specs=[SMEM] + [VMEM] * 2 + [HBM] * 7,
        out_specs=(HBM, VMEM, VMEM),
        scratch_shapes=[
            pltpu.VMEM((rows, chans), F32),
            pltpu.VMEM((rows, chans), F32),
            pltpu.VMEM((rows, chans), F32),
            pltpu.VMEM((rows, 128), F32),
            pltpu.VMEM((rows - frames, chans), F32),
            pltpu.VMEM((frames, 3 * chans), BF16),
            pltpu.VMEM((frames, chans), F32),
            pltpu.VMEM((frames, chans), BF16),
            pltpu.VMEM((rows, chans), F32),
            pltpu.VMEM((rows, chans), BF16),
            pltpu.VMEM((rows, chans), BF16),
            pltpu.VMEM((16, chans), F32),
            pltpu.VMEM((frames, chans), BF16),
            pltpu.VMEM((frames + 16, 128), F32),
            pltpu.VMEM((rows, 128), BF16),
            pltpu.VMEM((32, chans), F32),
            pltpu.VMEM((10, chans), F32),
            pltpu.VMEM((1, chans), F32),
            pltpu.VMEM((1, chans), F32),
            pltpu.VMEM((3 * chans, chans), BF16),
            pltpu.VMEM((1, chans), F32),
            pltpu.VMEM((1, chans), F32),
            pltpu.VMEM((frames, chans), BF16),
            pltpu.VMEM((frames, chans), BF16),
            pltpu.SemaphoreType.DMA((8,)),
        ],
        compiler_params=pltpu.CompilerParams(vmem_limit_bytes=32 << 20),
        name="step",
    )(
        lengths,
        waveform.reshape(frames, 10),
        rim,
        *(
            pltpu.with_memory_space_constraint(operand, pltpu.HBM)
            for operand in (
                conv0_weight,
                norm0_gain.reshape(1, chans),
                norm0_shift.reshape(1, chans),
                conv1_weight.reshape(3 * chans, chans),
                norm1_gain.reshape(1, chans),
                norm1_shift.reshape(1, chans),
                cotangent[0],
            )
        ),
    )
    mine = keep + lax.ppermute(send, "core", [(0, 1), (1, 0)])
    small_call = functools.partial(pl.pallas_call, compiler_params=pltpu.CompilerParams(vmem_limit_bytes=8 << 20))

    def stage(kernel, value, shapes, sums):
        return small_call(
            kernel,
            out_shape=[shape(s, F32) for s in shapes],
            in_specs=[VMEM],
            out_specs=[VMEM] * len(shapes),
            scratch_shapes=[pltpu.VMEM(sums, F32)],
            name=kernel.__name__,
        )(value)

    mine = lax.all_to_all(mine, AXES, 0, 0, axis_index_groups=cubes(), tiled=True)
    (mine,) = stage(cube_kernel, mine, [(32, 8, half)], (200, half))
    mine = lax.all_to_all(mine, FAR, 0, 0, tiled=True)
    (mine,) = stage(far_kernel, mine, [(32, 4, half)], (8, half))
    mine = lax.all_to_all(mine, LAST, 0, 0, tiled=True)
    conv1_grad, small_grads = stage(last_kernel, mine, [(3 * half,), (14, chans)], (16, 4, half))
    return (features[None], conv1_grad, small_grads)


def solution(mesh):
    torus = Mesh(mesh.devices.reshape(SHAPE), AXES)
    in_specs = (P(DP, AUDIO), P(DP), P(), P(), P(), P(), P(), P(), P(DP, AUDIO, None))
    out_specs = (P(DP, AUDIO, None), P(DP + AUDIO), P())
    return jax.shard_map(shards, mesh=torus, in_specs=in_specs, out_specs=out_specs, check_vma=False)
```

```python
import functools

import jax
import jax.numpy as jnp
import numpy as np
from jax import lax
from jax.experimental import pallas as pl
from jax.experimental.pallas import tpu as pltpu
from jax.sharding import Mesh
from jax.sharding import PartitionSpec as P

SHAPE = (2,) * 10
AXES = ("z2", "y2", "y1", "y0", "z1", "z0", "x2", "x1", "x0", "core")
DP, AUDIO = AXES[:4], AXES[4:]
CUBE = ("y0", "z0", "x0")
FAR = ("y2", "y1", "z1", "x2", "x1")
LAST = ("core", "y0", "z0", "x0", "z2")
GROUP = 384
EPS = 1e-05
BF16, F32 = jnp.bfloat16, jnp.float32


def cubes():
    groups = {}
    for i in range(2 ** len(AXES)):
        at = dict(zip(AXES, (int(v) for v in np.unravel_index(i, SHAPE))))
        group, member = [at["core"]], 0
        for axis in "yzx":
            place = sum(at[f"{axis}{n}"] << n for n in range(3))
            group.append((place - at["core"]) % 8 // 2)
            member = member * 2 + place % 2
        groups.setdefault(tuple(group), [0] * 8)[member] = i
    return list(groups.values())


def row_order(place):
    chunk = (place * 171) >> 9
    row = place - 3 * chunk
    for source, target in ((6, 5), (5, 3), (4, 0), (3, 6), (2, 4), (1, 2), (0, 1)):
        row = row + (((chunk >> source) & 1) << target) * 3
    return row


def normal_cdf(v):
    return 0.5 + 0.5 * lax.erf(v * np.float32(0.5**0.5))


def normal_pdf(v):
    return jnp.exp(v * v * np.float32(-0.5)) * np.float32((2 * np.pi) ** -0.5)


def fill_patches(block_ref, rim_ref, ext_ref, xs_ref, start, length):
    frames = block_ref.shape[0]
    row = lax.broadcasted_iota(jnp.int32, (frames, 10), 0)
    lane = lax.broadcasted_iota(jnp.int32, (frames, 10), 1)
    ext_ref[...] = jnp.zeros_like(ext_ref)
    ext_ref[0:frames, 0:10] = jnp.where(start + row * 10 + lane < length, block_ref[...], 0.0)
    lane = lax.broadcasted_iota(jnp.int32, (1, 128), 1)
    rim = jnp.where((lane < 10) & (start + frames * 10 + lane < length), rim_ref[:, :128], 0.0)
    ext_ref[frames : frames + 1] = rim
    here, after = ext_ref[...], ext_ref[1 : frames + 1]
    lane = lax.broadcasted_iota(jnp.int32, (frames, 128), 1)
    later = jnp.where(lane < 5, after, 0.0)
    odd = pltpu.roll(jnp.where(lane >= 5, here[:frames], 0.0), 123, 1) + pltpu.roll(later, 5, 1)
    for at, value in ((0, odd), (frames, here)):
        value = value + pltpu.roll(value, 10, 1) + pltpu.roll(value, 20, 1)
        high = value.astype(BF16).astype(F32)
        lane = lax.broadcasted_iota(jnp.int32, value.shape, 1)
        xs_ref[at : at + value.shape[0]] = jnp.where(lane < 20, high, value - high).astype(BF16)


def step_kernel(
    frames,
    chunk,
    length_ref,
    block_ref,
    rim_ref,
    w0_hbm,
    gain0_hbm,
    shift0_hbm,
    w1_hbm,
    gain1_hbm,
    shift1_hbm,
    cot_hbm,
    feat_hbm,
    keep_ref,
    send_ref,
    pre0_ref,
    xhat_ref,
    slope_ref,
    rstd_ref,
    even_ref,
    patch_ref,
    pre1_ref,
    d_ref,
    dact_ref,
    dhigh_ref,
    dlow_ref,
    small_ref,
    sides_ref,
    ext_ref,
    xs_ref,
    taps_ref,
    w0_ref,
    gain0_ref,
    shift0_ref,
    w1_ref,
    gain1_ref,
    shift1_ref,
    cot_ref,
    feat_ref,
    sems,
):
    arriving = []
    sources = (w0_hbm, gain0_hbm, shift0_hbm, w1_hbm, gain1_hbm, shift1_hbm, cot_hbm)
    targets = (w0_ref, gain0_ref, shift0_ref, w1_ref, gain1_ref, shift1_ref, cot_ref)
    for i, (source, target) in enumerate(zip(sources, targets)):
        arriving.append(pltpu.make_async_copy(source, target, sems.at[i]))
        arriving[-1].start()
    chans = w1_ref.shape[1]
    half = chans // 2
    rows = pre0_ref.shape[0]
    core = lax.axis_index("core")
    position = lax.axis_index(AUDIO)
    length = length_ref[0]
    fill_patches(block_ref, rim_ref, ext_ref, xs_ref, position * (frames * 10), length)
    xs = xs_ref[:, :30]
    arriving[0].wait()
    w0 = w0_ref[...]
    w0 = w0 - jnp.mean(w0, -1, keepdims=True)
    high = w0.astype(BF16).astype(F32)
    taps_ref[0:10] = high
    taps_ref[10:20] = w0 - high
    taps_ref[20:30] = high
    ws = taps_ref[0:30].astype(BF16)
    pre0_ref[...] = jnp.dot(xs, ws, preferred_element_type=F32)
    arriving[1].wait()
    arriving[2].wait()
    gain0 = jnp.broadcast_to(gain0_ref[...], (chunk, chans))
    shift0 = jnp.broadcast_to(shift0_ref[...], (chunk, chans))
    for at in range(0, rows, chunk):
        centred = pre0_ref[at : at + chunk]
        rstd = lax.rsqrt(jnp.mean(centred * centred, -1, keepdims=True) + EPS)
        xhat = centred * rstd
        v = xhat * gain0 + shift0
        cdf = normal_cdf(v)
        xhat_ref[at : at + chunk] = xhat
        slope_ref[at : at + chunk] = cdf + v * normal_pdf(v)
        rstd_ref[at : at + chunk] = jnp.broadcast_to(rstd, (chunk, 128))
        act = v * cdf
        if at < frames:
            patch_ref[at : at + chunk, chans : 2 * chans] = act.astype(BF16)
        else:
            even_ref[at - frames : at - frames + chunk] = act
    for at in range(0, frames, chunk):
        patch_ref[at : at + chunk, :chans] = even_ref[at : at + chunk].astype(BF16)
        patch_ref[at : at + chunk, 2 * chans :] = even_ref[at + 1 : at + 1 + chunk].astype(BF16)
    arriving[3].wait()
    pre1_ref[...] = jnp.dot(patch_ref[...], w1_ref[...], preferred_element_type=F32)
    for copy in arriving[4:]:
        copy.wait()
    source = lax.broadcasted_iota(jnp.int32, (GROUP, GROUP), 1)
    order = row_order(lax.broadcasted_iota(jnp.int32, (GROUP, 1), 0))
    place = (source == order).astype(F32).astype(BF16)
    columns = []
    for group in range(3 * chans // GROUP):
        lanes = patch_ref[:, group * GROUP : (group + 1) * GROUP]
        turned = lax.dot_general(place, lanes, (((1,), (1,)), ((), ())), preferred_element_type=F32)
        columns.append(turned.astype(BF16))
    gain1 = jnp.broadcast_to(gain1_ref[...], (chunk, chans))
    shift1 = jnp.broadcast_to(shift1_ref[...], (chunk, chans))
    sum_gain = jnp.zeros((chunk, chans), F32)
    sum_shift = jnp.zeros((chunk, chans), F32)
    for at in range(0, frames, chunk):
        pre = pre1_ref[at : at + chunk]
        centred = pre - jnp.mean(pre, -1, keepdims=True)
        rstd = lax.rsqrt(jnp.mean(centred * centred, -1, keepdims=True) + EPS)
        xhat = centred * rstd
        v = xhat * gain1 + shift1
        cdf = normal_cdf(v)
        frame = at + lax.broadcasted_iota(jnp.int32, (chunk, chans), 0)
        valid = (position * frames + frame) * 10 + 10 <= length
        feat_ref[at : at + chunk] = jnp.where(valid, v * cdf, 0.0).astype(BF16)
        dv = cot_ref[at : at + chunk].astype(F32) * (cdf + v * normal_pdf(v))
        dv = jnp.where(valid, dv, 0.0)
        sum_gain = sum_gain + dv * xhat
        sum_shift = sum_shift + dv
        dx = dv * gain1
        first = jnp.mean(dx, -1, keepdims=True)
        second = jnp.mean(dx * xhat, -1, keepdims=True)
        d = rstd * (dx - first - xhat * second)
        d_ref[at : at + chunk] = d.astype(BF16)
        left, right = d[:, :half], d[:, half:]
        sides_ref[at : at + chunk, :half] = jnp.where(core == 0, right, left).astype(BF16)
        sides_ref[at : at + chunk, half:] = jnp.where(core == 0, left, right).astype(BF16)
    leaving = pltpu.make_async_copy(feat_ref, feat_hbm, sems.at[7])
    leaving.start()
    small_ref[12:13] = jnp.sum(sum_gain, 0, keepdims=True)
    small_ref[13:14] = jnp.sum(sum_shift, 0, keepdims=True)
    small_ref[14:16] = jnp.zeros((2, chans), F32)

    part = GROUP // 8

    def second_gradient(group):
        grad = jnp.dot(columns[group], sides_ref[...], preferred_element_type=F32)
        for cube in range(8):
            block = grad[cube * part : (cube + 1) * part]
            send_ref[cube, group * part : (group + 1) * part] = block[:, :half]
            keep_ref[cube, group * part : (group + 1) * part] = block[:, half:]

    over_rows = (((0,), (0,)), ((), ()))

    def spread(tap):
        return lax.dot_general(
            d_ref[...],
            w1_ref[tap * chans : (tap + 1) * chans],
            (((1,), (1,)), ((), ())),
            preferred_element_type=F32,
        )

    dact_ref[:frames] = spread(1)
    dact_ref[frames : 2 * frames] = spread(0)
    dact_ref[2 * frames :] = jnp.zeros((rows - 2 * frames, chans), F32)
    dact_ref[frames + 1 : 2 * frames + 1] += spread(2)
    sum_gain = jnp.zeros((chunk, chans), F32)
    sum_shift = jnp.zeros((chunk, chans), F32)
    for at in range(0, rows, chunk):
        if at % (5 * chunk) == 0 and at // (5 * chunk) < len(columns):
            second_gradient(at // (5 * chunk))
        xhat = xhat_ref[at : at + chunk]
        dv = dact_ref[at : at + chunk] * slope_ref[at : at + chunk]
        sum_gain = sum_gain + dv * xhat
        sum_shift = sum_shift + dv
        dx = dv * gain0
        first = jnp.mean(dx, -1, keepdims=True)
        second = jnp.mean(dx * xhat, -1, keepdims=True)
        d = rstd_ref[at : at + chunk, :1] * (dx - first - xhat * second)
        high = d.astype(BF16)
        dhigh_ref[at : at + chunk] = high
        dlow_ref[at : at + chunk] = (d - high.astype(F32)).astype(BF16)
    by_high = lax.dot_general(xs, dhigh_ref[...], over_rows, preferred_element_type=F32)
    by_low = lax.dot_general(xs, dlow_ref[...], over_rows, preferred_element_type=F32)
    small_ref[0:10] = by_high[0:10] + by_high[20:30] + by_low[0:10]
    small_ref[10:11] = jnp.sum(sum_gain, 0, keepdims=True)
    small_ref[11:12] = jnp.sum(sum_shift, 0, keepdims=True)
    last = keep_ref.shape[1] - 8
    for out_ref, owner in ((keep_ref, core), (send_ref, 1 - core)):
        for cube in range(8):
            row = small_ref[pl.ds(8 * owner + cube, 1)]
            out_ref[cube, last : last + 1] = row[:, :half]
            out_ref[cube, last + 1 : last + 2] = row[:, half:]
            out_ref[cube, last + 2 :] = jnp.zeros((6, half), F32)
    leaving.wait()


def cube_kernel(cube_ref, out_ref, sum_ref):
    sum_ref[...] = jnp.sum(cube_ref[...], 0)
    for target in range(32):
        for place in range(2):
            at = place * 96 + 3 * target
            out_ref[target, 3 * place : 3 * place + 3] = sum_ref[at : at + 3]
        out_ref[target, 6:8] = sum_ref[192:194]


def far_kernel(far_ref, out_ref, sum_ref):
    sum_ref[...] = jnp.sum(far_ref[...], 0)
    small = sum_ref[6:8]
    for core in range(2):
        for place in range(2):
            at = 3 * place + core
            message = jnp.concatenate([small, sum_ref[at : at + 2]], 0)
            for cube in range(8):
                out_ref[core * 16 + cube * 2 + place] = message


def last_kernel(all_ref, grad_ref, small_ref, sum_ref):
    half = all_ref.shape[2]
    sum_ref[...] = jnp.sum(all_ref[...].reshape(16, 2, 4, half), 1)
    core, cube = lax.axis_index("core"), lax.axis_index(CUBE)
    own = sum_ref[core * 8 + cube]
    other = sum_ref[(1 - core) * 8 + cube]
    grad_ref[0:half] = own[2]
    grad_ref[half : 2 * half] = jnp.where(core == 0, other[2], other[3])
    grad_ref[2 * half :] = own[3]
    for row in range(14):
        small_ref[row : row + 1, :half] = sum_ref[row, 0:1]
        small_ref[row : row + 1, half:] = sum_ref[row, 1:2]


HBM = pl.BlockSpec(memory_space=pltpu.HBM)
VMEM = pl.BlockSpec(memory_space=pltpu.VMEM)
SMEM = pl.BlockSpec(memory_space=pltpu.SMEM)


def shards(
    waveform,
    lengths,
    conv0_weight,
    norm0_gain,
    norm0_shift,
    conv1_weight,
    norm1_gain,
    norm1_shift,
    cotangent,
):
    frames = waveform.shape[1] // 10
    chans = conv1_weight.shape[2]
    rows = 2 * frames + 16
    back = []
    for i in range(2 ** len(AXES)):
        if i % 2 ** len(AUDIO):
            back.append((i, i - 1))
    rim = lax.ppermute(waveform, AXES, back)
    half = chans // 2
    chunk = 16
    shape = jax.ShapeDtypeStruct
    features, keep, send = pl.pallas_call(
        functools.partial(step_kernel, frames, chunk),
        out_shape=(
            shape((frames, chans), BF16),
            shape((8, 200, half), F32),
            shape((8, 200, half), F32),
        ),
        in_specs=[SMEM] + [VMEM] * 2 + [HBM] * 7,
        out_specs=(HBM, VMEM, VMEM),
        scratch_shapes=[
            pltpu.VMEM((rows, chans), F32),
            pltpu.VMEM((rows, chans), F32),
            pltpu.VMEM((rows, chans), F32),
            pltpu.VMEM((rows, 128), F32),
            pltpu.VMEM((rows - frames, chans), F32),
            pltpu.VMEM((frames, 3 * chans), BF16),
            pltpu.VMEM((frames, chans), F32),
            pltpu.VMEM((frames, chans), BF16),
            pltpu.VMEM((rows, chans), F32),
            pltpu.VMEM((rows, chans), BF16),
            pltpu.VMEM((rows, chans), BF16),
            pltpu.VMEM((16, chans), F32),
            pltpu.VMEM((frames, chans), BF16),
            pltpu.VMEM((frames + 16, 128), F32),
            pltpu.VMEM((rows, 128), BF16),
            pltpu.VMEM((32, chans), F32),
            pltpu.VMEM((10, chans), F32),
            pltpu.VMEM((1, chans), F32),
            pltpu.VMEM((1, chans), F32),
            pltpu.VMEM((3 * chans, chans), BF16),
            pltpu.VMEM((1, chans), F32),
            pltpu.VMEM((1, chans), F32),
            pltpu.VMEM((frames, chans), BF16),
            pltpu.VMEM((frames, chans), BF16),
            pltpu.SemaphoreType.DMA((8,)),
        ],
        compiler_params=pltpu.CompilerParams(vmem_limit_bytes=32 << 20),
        name="step",
    )(
        lengths,
        waveform.reshape(frames, 10),
        rim,
        *(
            pltpu.with_memory_space_constraint(operand, pltpu.HBM)
            for operand in (
                conv0_weight,
                norm0_gain.reshape(1, chans),
                norm0_shift.reshape(1, chans),
                conv1_weight.reshape(3 * chans, chans),
                norm1_gain.reshape(1, chans),
                norm1_shift.reshape(1, chans),
                cotangent[0],
            )
        ),
    )
    mine = keep + lax.ppermute(send, "core", [(0, 1), (1, 0)])
    small_call = functools.partial(pl.pallas_call, compiler_params=pltpu.CompilerParams(vmem_limit_bytes=8 << 20))

    def stage(kernel, value, shapes, sums):
        return small_call(
            kernel,
            out_shape=[shape(s, F32) for s in shapes],
            in_specs=[VMEM],
            out_specs=[VMEM] * len(shapes),
            scratch_shapes=[pltpu.VMEM(sums, F32)],
            name=kernel.__name__,
        )(value)

    mine = lax.all_to_all(mine, AXES, 0, 0, axis_index_groups=cubes(), tiled=True)
    (mine,) = stage(cube_kernel, mine, [(32, 8, half)], (200, half))
    mine = lax.all_to_all(mine, FAR, 0, 0, tiled=True)
    (mine,) = stage(far_kernel, mine, [(32, 4, half)], (8, half))
    mine = lax.all_to_all(mine, LAST, 0, 0, tiled=True)
    conv1_grad, small_grads = stage(last_kernel, mine, [(3 * half,), (14, chans)], (16, 4, half))
    return (features[None], conv1_grad, small_grads)


def solution(mesh):
    torus = Mesh(mesh.devices.reshape(SHAPE), AXES)
    in_specs = (P(DP, AUDIO), P(DP), P(), P(), P(), P(), P(), P(), P(DP, AUDIO, None))
    out_specs = (P(DP, AUDIO, None), P(DP + AUDIO), P())
    return jax.shard_map(shards, mesh=torus, in_specs=in_specs, out_specs=out_specs, check_vma=False)
```

```python
import functools

import jax
import jax.numpy as jnp
import numpy as np
from jax import lax
from jax.experimental import pallas as pl
from jax.experimental.pallas import tpu as pltpu
from jax.sharding import Mesh
from jax.sharding import PartitionSpec as P

SHAPE = (2,) * 10
AXES = ("z2", "y2", "y1", "y0", "z1", "z0", "x2", "x1", "x0", "core")
DP, AUDIO = AXES[:4], AXES[4:]
CUBE = ("y0", "z0", "x0")
FAR = ("y2", "y1", "z1", "x2", "x1")
LAST = ("core", "y0", "z0", "x0", "z2")
GROUP = 384
EPS = 1e-05
BF16, F32 = jnp.bfloat16, jnp.float32


def cubes():
    groups = {}
    for i in range(2 ** len(AXES)):
        at = dict(zip(AXES, (int(v) for v in np.unravel_index(i, SHAPE))))
        group, member = [at["core"]], 0
        for axis in "yzx":
            place = sum(at[f"{axis}{n}"] << n for n in range(3))
            group.append((place - at["core"]) % 8 // 2)
            member = member * 2 + place % 2
        groups.setdefault(tuple(group), [0] * 8)[member] = i
    return list(groups.values())


def row_order(place):
    chunk = (place * 171) >> 9
    row = place - 3 * chunk
    for source, target in ((6, 5), (5, 3), (4, 0), (3, 6), (2, 4), (1, 2), (0, 1)):
        row = row + (((chunk >> source) & 1) << target) * 3
    return row


def normal_cdf(v):
    return 0.5 + 0.5 * lax.erf(v * np.float32(0.5**0.5))


def normal_pdf(v):
    return jnp.exp(v * v * np.float32(-0.5)) * np.float32((2 * np.pi) ** -0.5)


def fill_patches(block_ref, rim_ref, ext_ref, xs_ref, start, length):
    frames = block_ref.shape[0]
    row = lax.broadcasted_iota(jnp.int32, (frames, 10), 0)
    lane = lax.broadcasted_iota(jnp.int32, (frames, 10), 1)
    ext_ref[...] = jnp.zeros_like(ext_ref)
    ext_ref[0:frames, 0:10] = jnp.where(start + row * 10 + lane < length, block_ref[...], 0.0)
    lane = lax.broadcasted_iota(jnp.int32, (1, 128), 1)
    rim = jnp.where((lane < 10) & (start + frames * 10 + lane < length), rim_ref[:, :128], 0.0)
    ext_ref[frames : frames + 1] = rim
    here, after = ext_ref[...], ext_ref[1 : frames + 1]
    lane = lax.broadcasted_iota(jnp.int32, (frames, 128), 1)
    later = jnp.where(lane < 5, after, 0.0)
    odd = pltpu.roll(jnp.where(lane >= 5, here[:frames], 0.0), 123, 1) + pltpu.roll(later, 5, 1)
    for at, value in ((0, odd), (frames, here)):
        value = value + pltpu.roll(value, 10, 1) + pltpu.roll(value, 20, 1)
        high = value.astype(BF16).astype(F32)
        lane = lax.broadcasted_iota(jnp.int32, value.shape, 1)
        xs_ref[at : at + value.shape[0]] = jnp.where(lane < 20, high, value - high).astype(BF16)


def step_kernel(
    frames,
    chunk,
    length_ref,
    block_ref,
    rim_ref,
    w0_hbm,
    gain0_hbm,
    shift0_hbm,
    w1_hbm,
    gain1_hbm,
    shift1_hbm,
    cot_hbm,
    feat_hbm,
    keep_ref,
    send_ref,
    pre0_ref,
    xhat_ref,
    slope_ref,
    rstd_ref,
    even_ref,
    patch_ref,
    pre1_ref,
    d_ref,
    dact_ref,
    dhigh_ref,
    dlow_ref,
    small_ref,
    sides_ref,
    ext_ref,
    xs_ref,
    taps_ref,
    w0_ref,
    gain0_ref,
    shift0_ref,
    w1_ref,
    gain1_ref,
    shift1_ref,
    cot_ref,
    feat_ref,
    sems,
):
    arriving = []
    sources = (w0_hbm, gain0_hbm, shift0_hbm, w1_hbm, gain1_hbm, shift1_hbm, cot_hbm)
    targets = (w0_ref, gain0_ref, shift0_ref, w1_ref, gain1_ref, shift1_ref, cot_ref)
    for i, (source, target) in enumerate(zip(sources, targets)):
        arriving.append(pltpu.make_async_copy(source, target, sems.at[i]))
        arriving[-1].start()
    chans = w1_ref.shape[1]
    half = chans // 2
    rows = pre0_ref.shape[0]
    core = lax.axis_index("core")
    position = lax.axis_index(AUDIO)
    length = length_ref[0]
    fill_patches(block_ref, rim_ref, ext_ref, xs_ref, position * (frames * 10), length)
    xs = xs_ref[:, :30]
    arriving[0].wait()
    w0 = w0_ref[...]
    w0 = w0 - jnp.mean(w0, -1, keepdims=True)
    high = w0.astype(BF16).astype(F32)
    taps_ref[0:10] = high
    taps_ref[10:20] = w0 - high
    taps_ref[20:30] = high
    ws = taps_ref[0:30].astype(BF16)
    pre0_ref[...] = jnp.dot(xs, ws, preferred_element_type=F32)
    arriving[1].wait()
    arriving[2].wait()
    gain0 = jnp.broadcast_to(gain0_ref[...], (chunk, chans))
    shift0 = jnp.broadcast_to(shift0_ref[...], (chunk, chans))
    for at in range(0, rows, chunk):
        centred = pre0_ref[at : at + chunk]
        rstd = lax.rsqrt(jnp.mean(centred * centred, -1, keepdims=True) + EPS)
        xhat = centred * rstd
        v = xhat * gain0 + shift0
        cdf = normal_cdf(v)
        xhat_ref[at : at + chunk] = xhat
        slope_ref[at : at + chunk] = cdf + v * normal_pdf(v)
        rstd_ref[at : at + chunk] = jnp.broadcast_to(rstd, (chunk, 128))
        act = v * cdf
        if at < frames:
            patch_ref[at : at + chunk, chans : 2 * chans] = act.astype(BF16)
        else:
            even_ref[at - frames : at - frames + chunk] = act
    for at in range(0, frames, chunk):
        patch_ref[at : at + chunk, :chans] = even_ref[at : at + chunk].astype(BF16)
        patch_ref[at : at + chunk, 2 * chans :] = even_ref[at + 1 : at + 1 + chunk].astype(BF16)
    arriving[3].wait()
    pre1_ref[...] = jnp.dot(patch_ref[...], w1_ref[...], preferred_element_type=F32)
    for copy in arriving[4:]:
        copy.wait()
    source = lax.broadcasted_iota(jnp.int32, (GROUP, GROUP), 1)
    order = row_order(lax.broadcasted_iota(jnp.int32, (GROUP, 1), 0))
    place = (source == order).astype(F32).astype(BF16)
    columns = []

    def turn():
        lanes = patch_ref[:, len(columns) * GROUP : (len(columns) + 1) * GROUP]
        turned = lax.dot_general(place, lanes, (((1,), (1,)), ((), ())), preferred_element_type=F32)
        columns.append(turned.astype(BF16))

    gain1 = jnp.broadcast_to(gain1_ref[...], (chunk, chans))
    shift1 = jnp.broadcast_to(shift1_ref[...], (chunk, chans))
    sum_gain = jnp.zeros((chunk, chans), F32)
    sum_shift = jnp.zeros((chunk, chans), F32)
    for at in range(0, frames, chunk):
        if at % (3 * chunk) == 0:
            turn()
        pre = pre1_ref[at : at + chunk]
        centred = pre - jnp.mean(pre, -1, keepdims=True)
        rstd = lax.rsqrt(jnp.mean(centred * centred, -1, keepdims=True) + EPS)
        xhat = centred * rstd
        v = xhat * gain1 + shift1
        cdf = normal_cdf(v)
        frame = at + lax.broadcasted_iota(jnp.int32, (chunk, chans), 0)
        valid = (position * frames + frame) * 10 + 10 <= length
        feat_ref[at : at + chunk] = jnp.where(valid, v * cdf, 0.0).astype(BF16)
        dv = cot_ref[at : at + chunk].astype(F32) * (cdf + v * normal_pdf(v))
        dv = jnp.where(valid, dv, 0.0)
        sum_gain = sum_gain + dv * xhat
        sum_shift = sum_shift + dv
        dx = dv * gain1
        first = jnp.mean(dx, -1, keepdims=True)
        second = jnp.mean(dx * xhat, -1, keepdims=True)
        d = rstd * (dx - first - xhat * second)
        d_ref[at : at + chunk] = d.astype(BF16)
        left, right = d[:, :half], d[:, half:]
        sides_ref[at : at + chunk, :half] = jnp.where(core == 0, right, left).astype(BF16)
        sides_ref[at : at + chunk, half:] = jnp.where(core == 0, left, right).astype(BF16)
    leaving = pltpu.make_async_copy(feat_ref, feat_hbm, sems.at[7])
    leaving.start()
    small_ref[12:13] = jnp.sum(sum_gain, 0, keepdims=True)
    small_ref[13:14] = jnp.sum(sum_shift, 0, keepdims=True)
    small_ref[14:16] = jnp.zeros((2, chans), F32)

    part = GROUP // 8

    def second_gradient(group):
        grad = jnp.dot(columns[group], sides_ref[...], preferred_element_type=F32)
        for cube in range(8):
            block = grad[cube * part : (cube + 1) * part]
            send_ref[cube, group * part : (group + 1) * part] = block[:, :half]
            keep_ref[cube, group * part : (group + 1) * part] = block[:, half:]

    over_rows = (((0,), (0,)), ((), ()))

    def spread(tap):
        return lax.dot_general(
            d_ref[...],
            w1_ref[tap * chans : (tap + 1) * chans],
            (((1,), (1,)), ((), ())),
            preferred_element_type=F32,
        )

    dact_ref[:frames] = spread(1)
    dact_ref[frames : 2 * frames] = spread(0)
    dact_ref[2 * frames :] = jnp.zeros((rows - 2 * frames, chans), F32)
    dact_ref[frames + 1 : 2 * frames + 1] += spread(2)
    sum_gain = jnp.zeros((chunk, chans), F32)
    sum_shift = jnp.zeros((chunk, chans), F32)
    for at in range(0, rows, chunk):
        if at % (5 * chunk) == 0 and at // (5 * chunk) < len(columns):
            second_gradient(at // (5 * chunk))
        xhat = xhat_ref[at : at + chunk]
        dv = dact_ref[at : at + chunk] * slope_ref[at : at + chunk]
        sum_gain = sum_gain + dv * xhat
        sum_shift = sum_shift + dv
        dx = dv * gain0
        first = jnp.mean(dx, -1, keepdims=True)
        second = jnp.mean(dx * xhat, -1, keepdims=True)
        d = rstd_ref[at : at + chunk, :1] * (dx - first - xhat * second)
        high = d.astype(BF16)
        dhigh_ref[at : at + chunk] = high
        dlow_ref[at : at + chunk] = (d - high.astype(F32)).astype(BF16)
    by_high = lax.dot_general(xs, dhigh_ref[...], over_rows, preferred_element_type=F32)
    by_low = lax.dot_general(xs, dlow_ref[...], over_rows, preferred_element_type=F32)
    small_ref[0:10] = by_high[0:10] + by_high[20:30] + by_low[0:10]
    small_ref[10:11] = jnp.sum(sum_gain, 0, keepdims=True)
    small_ref[11:12] = jnp.sum(sum_shift, 0, keepdims=True)
    last = keep_ref.shape[1] - 8
    for out_ref, owner in ((keep_ref, core), (send_ref, 1 - core)):
        for cube in range(8):
            row = small_ref[pl.ds(8 * owner + cube, 1)]
            out_ref[cube, last : last + 1] = row[:, :half]
            out_ref[cube, last + 1 : last + 2] = row[:, half:]
            out_ref[cube, last + 2 :] = jnp.zeros((6, half), F32)
    leaving.wait()


def cube_kernel(cube_ref, out_ref, sum_ref):
    sum_ref[...] = jnp.sum(cube_ref[...], 0)
    for target in range(32):
        for place in range(2):
            at = place * 96 + 3 * target
            out_ref[target, 3 * place : 3 * place + 3] = sum_ref[at : at + 3]
        out_ref[target, 6:8] = sum_ref[192:194]


def far_kernel(far_ref, out_ref, sum_ref):
    sum_ref[...] = jnp.sum(far_ref[...], 0)
    small = sum_ref[6:8]
    for core in range(2):
        for place in range(2):
            at = 3 * place + core
            message = jnp.concatenate([small, sum_ref[at : at + 2]], 0)
            for cube in range(8):
                out_ref[core * 16 + cube * 2 + place] = message


def last_kernel(all_ref, grad_ref, small_ref, sum_ref):
    half = all_ref.shape[2]
    sum_ref[...] = jnp.sum(all_ref[...].reshape(16, 2, 4, half), 1)
    core, cube = lax.axis_index("core"), lax.axis_index(CUBE)
    own = sum_ref[core * 8 + cube]
    other = sum_ref[(1 - core) * 8 + cube]
    grad_ref[0:half] = own[2]
    grad_ref[half : 2 * half] = jnp.where(core == 0, other[2], other[3])
    grad_ref[2 * half :] = own[3]
    for row in range(14):
        small_ref[row : row + 1, :half] = sum_ref[row, 0:1]
        small_ref[row : row + 1, half:] = sum_ref[row, 1:2]


HBM = pl.BlockSpec(memory_space=pltpu.HBM)
VMEM = pl.BlockSpec(memory_space=pltpu.VMEM)
SMEM = pl.BlockSpec(memory_space=pltpu.SMEM)


def shards(
    waveform,
    lengths,
    conv0_weight,
    norm0_gain,
    norm0_shift,
    conv1_weight,
    norm1_gain,
    norm1_shift,
    cotangent,
):
    frames = waveform.shape[1] // 10
    chans = conv1_weight.shape[2]
    rows = 2 * frames + 16
    back = []
    for i in range(2 ** len(AXES)):
        if i % 2 ** len(AUDIO):
            back.append((i, i - 1))
    rim = lax.ppermute(waveform, AXES, back)
    half = chans // 2
    chunk = 16
    shape = jax.ShapeDtypeStruct
    features, keep, send = pl.pallas_call(
        functools.partial(step_kernel, frames, chunk),
        out_shape=(
            shape((frames, chans), BF16),
            shape((8, 200, half), F32),
            shape((8, 200, half), F32),
        ),
        in_specs=[SMEM] + [VMEM] * 2 + [HBM] * 7,
        out_specs=(HBM, VMEM, VMEM),
        scratch_shapes=[
            pltpu.VMEM((rows, chans), F32),
            pltpu.VMEM((rows, chans), F32),
            pltpu.VMEM((rows, chans), F32),
            pltpu.VMEM((rows, 128), F32),
            pltpu.VMEM((rows - frames, chans), F32),
            pltpu.VMEM((frames, 3 * chans), BF16),
            pltpu.VMEM((frames, chans), F32),
            pltpu.VMEM((frames, chans), BF16),
            pltpu.VMEM((rows, chans), F32),
            pltpu.VMEM((rows, chans), BF16),
            pltpu.VMEM((rows, chans), BF16),
            pltpu.VMEM((16, chans), F32),
            pltpu.VMEM((frames, chans), BF16),
            pltpu.VMEM((frames + 16, 128), F32),
            pltpu.VMEM((rows, 128), BF16),
            pltpu.VMEM((32, chans), F32),
            pltpu.VMEM((10, chans), F32),
            pltpu.VMEM((1, chans), F32),
            pltpu.VMEM((1, chans), F32),
            pltpu.VMEM((3 * chans, chans), BF16),
            pltpu.VMEM((1, chans), F32),
            pltpu.VMEM((1, chans), F32),
            pltpu.VMEM((frames, chans), BF16),
            pltpu.VMEM((frames, chans), BF16),
            pltpu.SemaphoreType.DMA((8,)),
        ],
        compiler_params=pltpu.CompilerParams(vmem_limit_bytes=32 << 20),
        name="step",
    )(
        lengths,
        waveform.reshape(frames, 10),
        rim,
        *(
            pltpu.with_memory_space_constraint(operand, pltpu.HBM)
            for operand in (
                conv0_weight,
                norm0_gain.reshape(1, chans),
                norm0_shift.reshape(1, chans),
                conv1_weight.reshape(3 * chans, chans),
                norm1_gain.reshape(1, chans),
                norm1_shift.reshape(1, chans),
                cotangent[0],
            )
        ),
    )
    mine = keep + lax.ppermute(send, "core", [(0, 1), (1, 0)])
    small_call = functools.partial(pl.pallas_call, compiler_params=pltpu.CompilerParams(vmem_limit_bytes=8 << 20))

    def stage(kernel, value, shapes, sums):
        return small_call(
            kernel,
            out_shape=[shape(s, F32) for s in shapes],
            in_specs=[VMEM],
            out_specs=[VMEM] * len(shapes),
            scratch_shapes=[pltpu.VMEM(sums, F32)],
            name=kernel.__name__,
        )(value)

    mine = lax.all_to_all(mine, AXES, 0, 0, axis_index_groups=cubes(), tiled=True)
    (mine,) = stage(cube_kernel, mine, [(32, 8, half)], (200, half))
    mine = lax.all_to_all(mine, FAR, 0, 0, tiled=True)
    (mine,) = stage(far_kernel, mine, [(32, 4, half)], (8, half))
    mine = lax.all_to_all(mine, LAST, 0, 0, tiled=True)
    conv1_grad, small_grads = stage(last_kernel, mine, [(3 * half,), (14, chans)], (16, 4, half))
    return (features[None], conv1_grad, small_grads)


def solution(mesh):
    torus = Mesh(mesh.devices.reshape(SHAPE), AXES)
    in_specs = (P(DP, AUDIO), P(DP), P(), P(), P(), P(), P(), P(), P(DP, AUDIO, None))
    out_specs = (P(DP, AUDIO, None), P(DP + AUDIO), P())
    return jax.shard_map(shards, mesh=torus, in_specs=in_specs, out_specs=out_specs, check_vma=False)
```
